32 devices in a mesh: patch: 8 (over z, x), lat: 4 (over y, core).
Axes of the slice: x: 2, y: 2, z: 4, core: 2. Of those that a mesh axis runs over, the one named last changes fastest.
Arguments:
- obs_values: bfloat16 [4096, 96], P(('patch', 'lat')), may hold values from -6 to 6
- obs_count: int32 [32, 32], P(('patch', 'lat')), may hold values from 0 to 4, as said below
- obs_node: int32 [4096, 3], P(('patch', 'lat')), may hold values from 0 to 319
- mesh_init: bfloat16 [10240, 512], P(('patch', 'lat')), may hold values from -6 to 6
- mesh_offset: int32 [10240, 6], P(('patch', 'lat')), may hold values from -128 to 128, as said below
- weights_flat: bfloat16 [32, 75264], P(('patch', 'lat')), may hold values from -0.25 to 0.25
- edge_bias: float32 [2, 512], replicated, may hold values from -3 to 3
- node_bias: float32 [2, 512], replicated, may hold values from -3 to 3
- norm_gain: float32 [2, 512], replicated, may hold values from 0.1 to 1.9
Outputs:
- mesh_latent: bfloat16 [10240, 512], P(('patch', 'lat'))
The draws below stay inside these ranges and needn't reach their ends.
Inputs may be any that keep to these rules, and one draw needn't show every extreme that they name: obs_count[s, d] counts the live slots (the first ones) among the 4 slots that device s holds for device d; each source fills all 4 slots for some destination, and some destination receives 4 live slots from every source. `obs_node`: local node on the destination device. The k-th incoming edge of node n comes from node (n + mesh_offset[n, k]) mod 10240; offsets of both -128 and 128 occur.
All inputs are finite; a program needn't handle non-finite values.
Results may differ from the reference program's by a relative error of at most 0.0085.
Values may be sent and summed in bfloat16 or wider, within the bound.
No kernel may reach another device: no remote copies, remote signals or barrier semaphores. Data moves between devices by JAX's collectives and lax.ppermute only.
A program may use at most 128 MiB of HBM per device.

```python
import jax
import jax.numpy as jnp
from jax import lax

D = 512
CH = 96
OBS_EDGES = 3
DEG = 6
HALO = 128
NODE_DEV = 320
CAP = 4
SENDERS = 32
SLOTS = 128
OBS_SLOTS = 4096
NODES = 10240
WROW = 75264


def draw_obs_count(key, part):
    first_key, second_key, third_key, fourth_key = jax.random.split(key, 4)
    base = jax.random.randint(first_key, (SENDERS, SENDERS), 0, CAP // 2 + 1)
    heat = jax.random.randint(second_key, (1, SENDERS), 1, 4)
    counts = jnp.minimum(base * heat, CAP)
    order = jax.random.permutation(third_key, SENDERS)
    columns = jnp.arange(SENDERS)[None, :]
    filled = columns == order[:, None]
    hottest = jax.random.randint(fourth_key, (), 0, SENDERS)
    filled = filled | (columns == hottest)
    return jnp.where(filled, CAP, counts).astype(jnp.int32)


def draw_mesh_offset(key, part):
    first_key, second_key, third_key = jax.random.split(key, 3)
    offsets = jax.random.randint(first_key, (NODES, DEG), -HALO, HALO + 1)
    picked = jax.random.randint(second_key, (NODES, 1), 0, 16) == 0
    signs = jax.random.randint(third_key, (NODES, 1), 0, 2) * 2 - 1
    leading = jnp.arange(DEG)[None, :] == 0
    return jnp.where(picked & leading, signs * HALO, offsets).astype(jnp.int32)


def with_ends(values, key, least, largest):
    longest = values.shape.index(max(values.shape))
    spots = []
    for shift in (0, 1):
        where = [jax.random.randint(jax.random.fold_in(key, axis), (), 0, length) for axis, length in enumerate(values.shape)]
        where[longest] = (where[longest] + shift) % values.shape[longest]
        spots.append(tuple(where))
    return values.at[spots[0]].set(least).at[spots[1]].set(largest)


def shard_levels(own_key, shape, cuts, smallest, high):
    def one(axis_at, shards_of):
        steps = jax.random.uniform(jax.random.fold_in(jax.random.fold_in(own_key, 6), axis_at), (shards_of,), jnp.float32, smallest / len(cuts), high / len(cuts))
        return jnp.repeat(jnp.exp(steps), shape[axis_at] // shards_of).reshape((-1,) + (1,) * (len(shape) - axis_at - 1))

    level = one(*cuts[0])
    for cut in cuts[1:]:
        level = level * one(*cut)
    return level


def scatter_about(own_key, dims, width, most, cuts=(), kind=jnp.bfloat16):
    result = width * jax.random.normal(own_key, dims, jnp.float32)
    if cuts:
        result = result * shard_levels(own_key, dims, cuts, -0.22, 0.18)
    return jnp.clip(result, -most, most).astype(kind)


def setup_inputs(seed: int = 0) -> dict:
    key_of = jax.random.split(jax.random.key(seed), 10)
    return {
        "obs_values": scatter_about(key_of[0], (OBS_SLOTS, CH), 1.0, 6.0, ((0, 32),)),
        "obs_count": draw_obs_count(jax.random.fold_in(key_of[9], 71), 0),
        "obs_node": with_ends(jax.random.randint(key_of[2], (OBS_SLOTS, OBS_EDGES), 0, NODE_DEV), jax.random.fold_in(key_of[2], 1), 0, NODE_DEV - 1).astype(jnp.int32),
        "mesh_init": scatter_about(key_of[3], (NODES, D), 1.0, 6.0, ((0, 32),)),
        "mesh_offset": draw_mesh_offset(jax.random.fold_in(key_of[9], 71), 0),
        "weights_flat": scatter_about(key_of[5], (SENDERS, WROW), D ** -0.5, 0.25, ((0, 32),)),
        "edge_bias": scatter_about(key_of[6], (2, D), 0.5, 3.0, (), jnp.float32),
        "node_bias": scatter_about(key_of[7], (2, D), 0.5, 3.0, (), jnp.float32),
        "norm_gain": jnp.clip(1.0 + 0.18 * jax.random.normal(key_of[8], (2, D), jnp.float32), 0.1, 1.9),
    }


def unpack(flat):
    shapes = ((CH, D), (D, 2 * D), (D, D), (D, D), (D, 3 * D), (D, D), (D, D))
    pieces = []
    offset = 0
    for height, breadth in shapes:
        pieces.append(flat[offset:offset + height * breadth].reshape(height, breadth))
        offset = offset + height * breadth
    return pieces

def layer_norm(values, gain):
    center = values - lax.optimization_barrier(jnp.mean(values, axis=-1, keepdims=True))
    spread = lax.optimization_barrier(jnp.mean(center * center, axis=-1, keepdims=True))
    return center * lax.rsqrt(spread + 1e-05) * gain

def reference(obs_values, obs_count, obs_node, mesh_init, mesh_offset, weights_flat, edge_bias, node_bias, norm_gain):
    w_in, w_enc, w_agg, w_out, w_proc, w_pagg, w_pout = unpack(weights_flat.reshape(-1))
    encoded = jnp.dot(mesh_init, w_enc, preferred_element_type=jnp.float32)
    query = encoded[:, :D] + edge_bias[0]
    values = obs_values.reshape(SENDERS, SLOTS, CH)
    targets = obs_node.reshape(SENDERS, SLOTS, OBS_EDGES)
    slot_ids = jnp.arange(SLOTS, dtype=jnp.int32)
    destin = slot_ids // CAP
    position = slot_ids % CAP

    def one_source(totals, inputs):
        rows, nodes, counts = inputs
        embedded = jnp.dot(rows, w_in, preferred_element_type=jnp.float32).astype(jnp.bfloat16)
        alive = (position < counts[destin]).astype(jnp.float32)[:, None]
        global_ids = destin[:, None] * NODE_DEV + nodes
        for which in range(OBS_EDGES):
            message = jax.nn.silu(embedded.astype(jnp.float32) + query[global_ids[:, which]]) * alive
            totals = totals.at[global_ids[:, which]].add(message)
        return (totals, None)
    totals, _ = lax.scan(one_source, jnp.zeros((NODES, D), jnp.float32), (values, targets, obs_count))
    gathered = totals.astype(jnp.bfloat16)
    hidden = jax.nn.silu(encoded[:, D:] + jnp.dot(gathered, w_agg, preferred_element_type=jnp.float32) + node_bias[0]).astype(jnp.bfloat16)
    first = (mesh_init.astype(jnp.float32) + layer_norm(jnp.dot(hidden, w_out, preferred_element_type=jnp.float32), norm_gain[0])).astype(jnp.bfloat16)
    projected = jnp.dot(first, w_proc, preferred_element_type=jnp.float32)
    sources = projected[:, :D].astype(jnp.bfloat16)
    target = projected[:, D:2 * D] + edge_bias[1]
    node_ids = jnp.arange(NODES, dtype=jnp.int32)
    pooled = jnp.zeros((NODES, D), jnp.float32)
    for which in range(DEG):
        anchor = (node_ids + mesh_offset[:, which]) % NODES
        pooled = pooled + jax.nn.silu(sources[anchor].astype(jnp.float32) + target)
    hidden2 = jax.nn.silu(projected[:, 2 * D:] + jnp.dot(pooled.astype(jnp.bfloat16), w_pagg, preferred_element_type=jnp.float32) + node_bias[1]).astype(jnp.bfloat16)
    return (first.astype(jnp.float32) + layer_norm(jnp.dot(hidden2, w_pout, preferred_element_type=jnp.float32), norm_gain[1])).astype(jnp.bfloat16)
```

```python
import jax
import jax.numpy as jnp
from jax import lax
from jax.experimental import pallas as pl
from jax.experimental.pallas import tpu as pltpu
from jax.sharding import PartitionSpec as P

D = 512
CH = 96
OBS_EDGES = 3
DEG = 6
HALO = 128


def extended(block, sides, width):
    for axis, dim in sides:
        count = lax.axis_size(axis)
        forward = [(i, i + 1) for i in range(count - 1)]
        forward.append((count - 1, 0))
        backward = [(target, source) for source, target in forward]
        low = lax.ppermute(
            lax.slice_in_dim(block, block.shape[dim] - width, None, axis=dim), axis, forward
        )
        high = lax.ppermute(lax.slice_in_dim(block, 0, width, axis=dim), axis, backward)
        block = jnp.concatenate([low, block, high], axis=dim)
    return block


def unpack(flat):
    shapes = ((CH, D), (D, 2 * D), (D, D), (D, D), (D, 3 * D), (D, D), (D, D))
    pieces = []
    offset = 0
    for height, breadth in shapes:
        pieces.append(flat[offset : offset + height * breadth].reshape(height, breadth))
        offset = offset + height * breadth
    return pieces


def layer_norm(values, gain):
    center = values - jnp.mean(values, axis=-1, keepdims=True)
    spread = jnp.mean(center * center, axis=-1, keepdims=True)
    return center * lax.rsqrt(spread + 1e-05) * gain


def embed_rows(rows, w_in):
    return jnp.dot(rows, w_in, preferred_element_type=jnp.float32).astype(jnp.bfloat16)


def deliver(values, nodes, counts):
    return (
        lax.all_to_all(
            lax.all_to_all(values, "patch", split_axis=0, concat_axis=0, tiled=True),
            "lat",
            split_axis=1,
            concat_axis=1,
            tiled=True,
        ),
        lax.all_to_all(
            lax.all_to_all(nodes, "patch", split_axis=0, concat_axis=0, tiled=True),
            "lat",
            split_axis=1,
            concat_axis=1,
            tiled=True,
        ),
        lax.all_to_all(
            lax.all_to_all(counts, "patch", split_axis=0, concat_axis=0, tiled=True),
            "lat",
            split_axis=1,
            concat_axis=1,
            tiled=True,
        ),
    )


def general(
    obs_values,
    obs_count,
    obs_node,
    mesh_init,
    mesh_offset,
    weights_flat,
    edge_bias,
    node_bias,
    norm_gain,
):
    n_patch = lax.axis_size("patch")
    n_lat = lax.axis_size("lat")
    senders = n_patch * n_lat
    capacity = obs_values.shape[0] // senders
    node_dev = mesh_init.shape[0]
    table = lax.all_gather(weights_flat, ("patch", "lat"), axis=0, tiled=True)
    w_in, w_enc, w_agg, w_out, w_proc, w_pagg, w_pout = unpack(table.reshape(-1))
    breadth = obs_values.shape[1]
    arrived, targets, counts = deliver(
        obs_values.reshape(n_patch, n_lat, capacity, breadth),
        obs_node.reshape(n_patch, n_lat, capacity, OBS_EDGES),
        obs_count.reshape(n_patch, n_lat),
    )
    arrived = arrived.reshape(senders * capacity, breadth)
    targets = targets.reshape(senders * capacity, OBS_EDGES)
    embedded = embed_rows(arrived, w_in)
    alive = (
        (jnp.arange(capacity, dtype=jnp.int32)[None, :] < counts.reshape(senders, 1))
        .astype(jnp.float32)
        .reshape(-1)
    )
    encoded = jnp.dot(mesh_init, w_enc, preferred_element_type=jnp.float32)
    query = encoded[:, :D] + edge_bias[0]
    total_rows = senders * capacity
    block = min(512, total_rows)
    turns = total_rows // block
    node_ids = jnp.arange(node_dev, dtype=jnp.int32)[None, :]

    def encode_block(block_index, totals):
        start = block_index * block
        piece = lax.dynamic_slice_in_dim(embedded, start, block, 0).astype(jnp.float32)
        nodes = lax.dynamic_slice_in_dim(targets, start, block, 0)
        weight = lax.dynamic_slice_in_dim(alive, start, block, 0)[:, None]
        for which in range(OBS_EDGES):
            selector = (nodes[:, which][:, None] == node_ids).astype(jnp.float32)
            picked = jnp.dot(selector, query, precision=lax.Precision.HIGHEST)
            message = jax.nn.silu(piece + picked) * weight
            totals = totals + lax.dot_general(
                selector, message, (((0,), (0,)), ((), ())), precision=lax.Precision.HIGHEST
            )
        return totals

    totals = lax.fori_loop(0, turns, encode_block, jnp.zeros((node_dev, D), jnp.float32))
    gathered = totals.astype(jnp.bfloat16)
    hidden = jax.nn.silu(
        encoded[:, D:] + jnp.dot(gathered, w_agg, preferred_element_type=jnp.float32) + node_bias[0]
    ).astype(jnp.bfloat16)
    first = (
        mesh_init.astype(jnp.float32)
        + layer_norm(jnp.dot(hidden, w_out, preferred_element_type=jnp.float32), norm_gain[0])
    ).astype(jnp.bfloat16)
    projected = jnp.dot(first, w_proc, preferred_element_type=jnp.float32)
    sources = projected[:, :D].astype(jnp.bfloat16)
    target = projected[:, D : 2 * D] + edge_bias[1]
    padded = extended(sources, ((("patch", "lat"), 0),), HALO)
    local_ids = jnp.arange(node_dev, dtype=jnp.int32) + HALO
    pooled = jnp.zeros((node_dev, D), jnp.float32)
    for which in range(DEG):
        anchor = local_ids + mesh_offset[:, which]
        pooled = pooled + jax.nn.silu(jnp.take(padded, anchor, axis=0).astype(jnp.float32) + target)
    hidden2 = jax.nn.silu(
        projected[:, 2 * D :]
        + jnp.dot(pooled.astype(jnp.bfloat16), w_pagg, preferred_element_type=jnp.float32)
        + node_bias[1]
    ).astype(jnp.bfloat16)
    return (
        first.astype(jnp.float32)
        + layer_norm(jnp.dot(hidden2, w_pout, preferred_element_type=jnp.float32), norm_gain[1])
    ).astype(jnp.bfloat16)


BF = jnp.bfloat16
F32 = jnp.float32
TILE = 16
FRAME = 168


def silu(values):
    half = 0.5 * values
    return half + half * jnp.tanh(half)


def mm(left, right):
    return jnp.dot(left, right, preferred_element_type=F32)


def iota(shape, dim):
    return lax.broadcasted_iota(jnp.int32, shape, dim)


def in_vmem():
    return pl.BlockSpec(memory_space=pltpu.VMEM)


def in_smem():
    return pl.BlockSpec(memory_space=pltpu.SMEM)


def in_any():
    return pl.BlockSpec(memory_space=pl.ANY)


def frame_kernel(me_ref, w_ref, val_ref, node_ref, count_ref, *refs):
    outs, (slots, rows, frame) = refs[:4], refs[4:]
    me = me_ref[0]
    height = w_ref.shape[0]
    n_slots, breadth = val_ref.shape
    senders = count_ref.shape[1]
    capacity = n_slots // senders
    phase = lax.rem(height * me, TILE)
    own = iota((n_slots, senders), 0) // capacity == iota((n_slots, senders), 1)
    live = jnp.sum(jnp.where(own, count_ref[...].astype(F32), 0.0), axis=1, keepdims=True)
    place = (iota((n_slots, 1), 0) % capacity).astype(F32)
    code = jnp.where(place < live, node_ref[...] + 1, 0)
    high = (code >> 4).astype(F32)
    low = (code & 15).astype(F32)
    lane = iota((n_slots, 128 - breadth), 1)
    tail = jnp.zeros((n_slots, 128 - breadth), F32)
    for k in range(OBS_EDGES):
        tail = jnp.where(lane == 2 * k, high[:, k : k + 1], tail)
        tail = jnp.where(lane == 2 * k + 1, low[:, k : k + 1], tail)
    slots[:, :breadth] = val_ref[...].astype(F32)
    slots[:, breadth:] = tail
    for j in range(capacity):
        rows[:, 128 * j : 128 * (j + 1)] = slots[pl.ds(j, senders, stride=capacity), :]
    shift = (iota((FRAME, height), 0) == iota((FRAME, height), 1) + phase).astype(BF)
    frame[...] = mm(shift, w_ref[...])
    start = pl.multiple_of(jnp.where(phase >= 8, 0, FRAME - 8), 8)
    for flip in range(4):
        plane = (me >> 3) ^ flip
        frame[pl.ds(start, 8), :] = rows[pl.ds(pl.multiple_of(plane * 8, 8), 8), :]
        outs[flip][...] = frame[...].astype(BF)


def encoder_kernel(me_ref, *refs):
    pieces = refs[:16]
    init_ref, edge_ref, nbias_ref, gain_ref = refs[16:20]
    src_ref, tgt_ref, rest_ref, first_ref, pagg_ref, pout_ref = refs[20:26]
    big, heads, tails, obs, enc, proc, sems = refs[26:]
    height = WROWS
    me = me_ref[0]
    core = me & 1
    copies = []
    at = 0
    for unit in range(4):
        for twin in range(2):
            ax = jnp.where((core ^ twin) == 0, 4, 2)
            ay = jnp.where((core ^ twin) == 0, 2, 4)
            for pair in range(2):
                for j in range(2):
                    piece = pieces[unit * 4 + twin * 2 + pair]
                    mask = (8 * unit) ^ twin ^ (ax if j else 0) ^ (ay if pair else 0)
                    dev = me ^ mask
                    row = pl.multiple_of((height * dev) // TILE * TILE + TILE, TILE)
                    for s, (lo, hi, dst) in enumerate((
                        (0, 16, heads.at[dev]),
                        (16, 144, big.at[pl.ds(row, 128)]),
                        (144, FRAME, tails.at[dev, pl.ds(0, FRAME - 144)]),
                    )):
                        copy = pltpu.make_async_copy(piece.at[j, pl.ds(lo, hi - lo)], dst, sems.at[at, s])
                        copy.start()
                        copies.append(copy)
                    at += 1
    for copy in copies:
        copy.wait()
    row16 = iota((TILE, D), 0)
    for dev in range(32):
        phase = height * dev % TILE
        tile = height * dev // TILE
        after = height * (dev + 1) // TILE
        head = heads[dev]
        if phase:
            before = height * (dev - 1) // TILE
            skip = TILE * (tile - before) - 144
            last = tails[dev - 1, skip : skip + TILE, :]
            head = jnp.where(row16 < phase, last.astype(F32), head.astype(F32)).astype(BF)
        big[TILE * tile : TILE * (tile + 1), :] = head
        if after - tile == 10:
            big[TILE * (tile + 9) : TILE * (tile + 10), :] = tails[dev, 0:TILE, :]
        if phase >= 8:
            seen = heads[dev].astype(F32)[0:8]
        else:
            seen = tails[dev, TILE : 2 * TILE, :].astype(F32)[0:8]
        for j in range(4):
            obs[j, 8 * dev : 8 * (dev + 1), :] = seen[:, 128 * j : 128 * (j + 1)]
    e0 = CH
    a0 = CH + 2 * D
    o0 = CH + 3 * D
    p0 = CH + 4 * D
    g0 = CH + 7 * D
    u0 = CH + 8 * D
    pagg_ref[...] = big[g0 : g0 + D, :]
    pout_ref[...] = big[u0 : u0 + D, :]
    out = iota((256, 256), 0)
    two = (iota((256, 256), 1) == 2 * (out & 127) + (out >> 7)).astype(BF)
    for j in range(D // 128):
        got = mm(two, big[e0 + 256 * j : e0 + 256 * (j + 1), :]).astype(BF)
        enc[0, 128 * j : 128 * (j + 1), :] = got[:128]
        enc[1, 128 * j : 128 * (j + 1), :] = got[128:]
    out = iota((384, 384), 0)
    three = (iota((384, 384), 1) == 3 * (out & 127) + (out >> 7)).astype(BF)
    for j in range(D // 128):
        got = mm(three, big[p0 + 384 * j : p0 + 384 * (j + 1), :]).astype(BF)
        for m in range(3):
            proc[m, 128 * j : 128 * (j + 1), :] = got[128 * m : 128 * (m + 1)]
    init = init_ref[...]
    query = mm(init, enc[0]) + edge_ref[0:1, :]
    slots = jnp.concatenate([obs[j, pl.ds(me & 7, 32, stride=8), :] for j in range(4)], axis=0)
    embedded = mm(slots[:, :CH].astype(BF), big[0:CH, :]).astype(BF).astype(F32)
    node_ids = iota((slots.shape[0], init.shape[0]), 1)
    picks = []
    for k in range(OBS_EDGES):
        code = slots[:, CH + 2 * k : CH + 2 * k + 1] * 16.0 + slots[:, CH + 2 * k + 1 : CH + 2 * k + 2]
        picks.append((node_ids == code.astype(jnp.int32) - 1).astype(F32))
    select = jnp.concatenate(picks, axis=0)
    spread = select.astype(BF)
    q_high = query.astype(BF)
    q_low = (query - q_high.astype(F32)).astype(BF)
    picked = mm(spread, q_high) + mm(spread, q_low)
    message = silu(jnp.concatenate([embedded] * OBS_EDGES, axis=0) + picked)
    collect = select.T.astype(BF)
    m_high = message.astype(BF)
    m_low = (message - m_high.astype(F32)).astype(BF)
    gathered = (mm(collect, m_high) + mm(collect, m_low)).astype(BF)
    hidden = silu(
        mm(init, enc[1]) + mm(gathered, big[a0 : a0 + D, :]) + nbias_ref[0:1, :]
    ).astype(BF)
    first = (
        init.astype(F32) + layer_norm(mm(hidden, big[o0 : o0 + D, :]), gain_ref[0:1, :])
    ).astype(BF)
    first_ref[...] = first
    src_ref[...] = mm(first, proc[0]).astype(BF)
    tgt_ref[...] = mm(first, proc[1]) + edge_ref[1:2, :]
    rest_ref[...] = mm(first, proc[2]) + nbias_ref[1:2, :]


def processor_kernel(
    low_ref, src_ref, high_ref, tgt_ref, rest_ref, first_ref, off_ref, pagg_ref, pout_ref, gain_ref, out_ref, ext
):
    count = src_ref.shape[0]
    ext[0:HALO, :] = low_ref[...]
    ext[HALO : HALO + count, :] = src_ref[...]
    ext[HALO + count :, :] = high_ref[...]
    target = tgt_ref[...]
    cols = iota((count, count + 2 * HALO), 1) - iota((count, count + 2 * HALO), 0) - HALO
    pooled = jnp.zeros((count, D), F32)
    for k in range(DEG):
        select = (cols == off_ref[:, k : k + 1]).astype(BF)
        pooled = pooled + silu(mm(select, ext[...]) + target)
    hidden = silu(rest_ref[...] + mm(pooled.astype(BF), pagg_ref[...])).astype(BF)
    out_ref[...] = (
        first_ref[...].astype(F32) + layer_norm(mm(hidden, pout_ref[...]), gain_ref[1:2, :])
    ).astype(BF)


WROWS = 147


def fits(obs_values, obs_node, mesh_init, weights_flat):
    return (
        lax.axis_size("patch") == 8
        and lax.axis_size("lat") == 4
        and weights_flat.shape[1] == WROWS * D
        and obs_values.shape == (128, CH)
        and mesh_init.shape[0] <= 320
        and mesh_init.shape[0] >= HALO
    )


def spread_weights(frames):
    axes = ("patch", "lat")

    def move(block, masks):
        return lax.ppermute(block, axes, [(i, i ^ masks[i & 1]) for i in range(32)])

    units = [frames[0]] + [move(frames[f], (8 * f, 8 * f)) for f in (1, 2, 3)]
    pieces = []
    for unit in units:
        pair = jnp.stack([unit, move(unit, (4, 2))])
        other = move(pair, (2, 4))
        pieces += [pair, other, move(pair, (1, 1)), move(other, (1, 1))]
    return pieces


def shards(
    obs_values,
    obs_count,
    obs_node,
    mesh_init,
    mesh_offset,
    weights_flat,
    edge_bias,
    node_bias,
    norm_gain,
):
    if not fits(obs_values, obs_node, mesh_init, weights_flat):
        return general(
            obs_values,
            obs_count,
            obs_node,
            mesh_init,
            mesh_offset,
            weights_flat,
            edge_bias,
            node_bias,
            norm_gain,
        )
    axes = ("patch", "lat")
    me = lax.axis_index(axes).astype(jnp.int32).reshape(1)
    count = mesh_init.shape[0]
    frames = pl.pallas_call(
        frame_kernel,
        out_shape=[jax.ShapeDtypeStruct((FRAME, D), BF)] * 4,
        in_specs=[in_smem()] + [in_vmem()] * 4,
        out_specs=[in_vmem()] * 4,
        scratch_shapes=[
            pltpu.VMEM((128, 128), F32),
            pltpu.VMEM((32, D), F32),
            pltpu.VMEM((FRAME, D), F32),
        ],
        name="frames",
    )(me, weights_flat.reshape(WROWS, D), obs_values, obs_node, obs_count)
    pieces = spread_weights(frames)
    wide = jax.ShapeDtypeStruct((count, D), F32)
    slim = jax.ShapeDtypeStruct((count, D), BF)
    square = jax.ShapeDtypeStruct((D, D), BF)
    sources, target, rest, first, w_pagg, w_pout = pl.pallas_call(
        encoder_kernel,
        out_shape=[slim, wide, wide, slim, square, square],
        in_specs=[in_smem()] + [in_any()] * 16 + [in_vmem()] * 4,
        out_specs=[in_vmem()] * 6,
        scratch_shapes=[
            pltpu.VMEM((32 * WROWS, D), BF),
            pltpu.VMEM((32, TILE, D), BF),
            pltpu.VMEM((32, 2 * TILE, D), BF),
            pltpu.VMEM((4, 256, 128), F32),
            pltpu.VMEM((2, D, D), BF),
            pltpu.VMEM((3, D, D), BF),
            pltpu.SemaphoreType.DMA((32, 3)),
        ],
        name="encoder",
    )(me, *pieces, mesh_init, edge_bias, node_bias, norm_gain)
    forward = [(i, (i + 1) % 32) for i in range(32)]
    backward = [(j, i) for i, j in forward]
    low = lax.ppermute(sources[count - HALO :], axes, forward)
    high = lax.ppermute(sources[:HALO], axes, backward)
    return pl.pallas_call(
        processor_kernel,
        out_shape=slim,
        in_specs=[in_vmem()] * 10,
        out_specs=in_vmem(),
        scratch_shapes=[pltpu.VMEM((count + 2 * HALO, D), BF)],
        name="processor",
    )(low, sources, high, target, rest, first, mesh_offset, w_pagg, w_pout, norm_gain)


def solution(mesh):
    return jax.shard_map(
        shards,
        mesh=mesh,
        in_specs=(
            P(("patch", "lat"), None),
            P(("patch", "lat"), None),
            P(("patch", "lat"), None),
            P(("patch", "lat"), None),
            P(("patch", "lat"), None),
            P(("patch", "lat"), None),
            P(),
            P(),
            P(),
        ),
        out_specs=P(("patch", "lat"), None),
        check_vma=False,
    )
```

```python
import jax
import jax.numpy as jnp
from jax import lax
from jax.experimental import pallas as pl
from jax.experimental.pallas import tpu as pltpu
from jax.sharding import PartitionSpec as P

D = 512
CH = 96
OBS_EDGES = 3
DEG = 6
HALO = 128


def extended(block, sides, width):
    for axis, dim in sides:
        count = lax.axis_size(axis)
        forward = [(i, i + 1) for i in range(count - 1)]
        forward.append((count - 1, 0))
        backward = [(target, source) for source, target in forward]
        low = lax.ppermute(
            lax.slice_in_dim(block, block.shape[dim] - width, None, axis=dim), axis, forward
        )
        high = lax.ppermute(lax.slice_in_dim(block, 0, width, axis=dim), axis, backward)
        block = jnp.concatenate([low, block, high], axis=dim)
    return block


def unpack(flat):
    shapes = ((CH, D), (D, 2 * D), (D, D), (D, D), (D, 3 * D), (D, D), (D, D))
    pieces = []
    offset = 0
    for height, breadth in shapes:
        pieces.append(flat[offset : offset + height * breadth].reshape(height, breadth))
        offset = offset + height * breadth
    return pieces


def layer_norm(values, gain):
    center = values - jnp.mean(values, axis=-1, keepdims=True)
    spread = jnp.mean(center * center, axis=-1, keepdims=True)
    return center * lax.rsqrt(spread + 1e-05) * gain


def embed_rows(rows, w_in):
    return jnp.dot(rows, w_in, preferred_element_type=jnp.float32).astype(jnp.bfloat16)


def deliver(values, nodes, counts):
    return (
        lax.all_to_all(
            lax.all_to_all(values, "patch", split_axis=0, concat_axis=0, tiled=True),
            "lat",
            split_axis=1,
            concat_axis=1,
            tiled=True,
        ),
        lax.all_to_all(
            lax.all_to_all(nodes, "patch", split_axis=0, concat_axis=0, tiled=True),
            "lat",
            split_axis=1,
            concat_axis=1,
            tiled=True,
        ),
        lax.all_to_all(
            lax.all_to_all(counts, "patch", split_axis=0, concat_axis=0, tiled=True),
            "lat",
            split_axis=1,
            concat_axis=1,
            tiled=True,
        ),
    )


def general(
    obs_values,
    obs_count,
    obs_node,
    mesh_init,
    mesh_offset,
    weights_flat,
    edge_bias,
    node_bias,
    norm_gain,
):
    n_patch = lax.axis_size("patch")
    n_lat = lax.axis_size("lat")
    senders = n_patch * n_lat
    capacity = obs_values.shape[0] // senders
    node_dev = mesh_init.shape[0]
    table = lax.all_gather(weights_flat, ("patch", "lat"), axis=0, tiled=True)
    w_in, w_enc, w_agg, w_out, w_proc, w_pagg, w_pout = unpack(table.reshape(-1))
    breadth = obs_values.shape[1]
    arrived, targets, counts = deliver(
        obs_values.reshape(n_patch, n_lat, capacity, breadth),
        obs_node.reshape(n_patch, n_lat, capacity, OBS_EDGES),
        obs_count.reshape(n_patch, n_lat),
    )
    arrived = arrived.reshape(senders * capacity, breadth)
    targets = targets.reshape(senders * capacity, OBS_EDGES)
    embedded = embed_rows(arrived, w_in)
    alive = (
        (jnp.arange(capacity, dtype=jnp.int32)[None, :] < counts.reshape(senders, 1))
        .astype(jnp.float32)
        .reshape(-1)
    )
    encoded = jnp.dot(mesh_init, w_enc, preferred_element_type=jnp.float32)
    query = encoded[:, :D] + edge_bias[0]
    total_rows = senders * capacity
    block = min(512, total_rows)
    turns = total_rows // block
    node_ids = jnp.arange(node_dev, dtype=jnp.int32)[None, :]

    def encode_block(block_index, totals):
        start = block_index * block
        piece = lax.dynamic_slice_in_dim(embedded, start, block, 0).astype(jnp.float32)
        nodes = lax.dynamic_slice_in_dim(targets, start, block, 0)
        weight = lax.dynamic_slice_in_dim(alive, start, block, 0)[:, None]
        for which in range(OBS_EDGES):
            selector = (nodes[:, which][:, None] == node_ids).astype(jnp.float32)
            picked = jnp.dot(selector, query, precision=lax.Precision.HIGHEST)
            message = jax.nn.silu(piece + picked) * weight
            totals = totals + lax.dot_general(
                selector, message, (((0,), (0,)), ((), ())), precision=lax.Precision.HIGHEST
            )
        return totals

    totals = lax.fori_loop(0, turns, encode_block, jnp.zeros((node_dev, D), jnp.float32))
    gathered = totals.astype(jnp.bfloat16)
    hidden = jax.nn.silu(
        encoded[:, D:] + jnp.dot(gathered, w_agg, preferred_element_type=jnp.float32) + node_bias[0]
    ).astype(jnp.bfloat16)
    first = (
        mesh_init.astype(jnp.float32)
        + layer_norm(jnp.dot(hidden, w_out, preferred_element_type=jnp.float32), norm_gain[0])
    ).astype(jnp.bfloat16)
    projected = jnp.dot(first, w_proc, preferred_element_type=jnp.float32)
    sources = projected[:, :D].astype(jnp.bfloat16)
    target = projected[:, D : 2 * D] + edge_bias[1]
    padded = extended(sources, ((("patch", "lat"), 0),), HALO)
    local_ids = jnp.arange(node_dev, dtype=jnp.int32) + HALO
    pooled = jnp.zeros((node_dev, D), jnp.float32)
    for which in range(DEG):
        anchor = local_ids + mesh_offset[:, which]
        pooled = pooled + jax.nn.silu(jnp.take(padded, anchor, axis=0).astype(jnp.float32) + target)
    hidden2 = jax.nn.silu(
        projected[:, 2 * D :]
        + jnp.dot(pooled.astype(jnp.bfloat16), w_pagg, preferred_element_type=jnp.float32)
        + node_bias[1]
    ).astype(jnp.bfloat16)
    return (
        first.astype(jnp.float32)
        + layer_norm(jnp.dot(hidden2, w_pout, preferred_element_type=jnp.float32), norm_gain[1])
    ).astype(jnp.bfloat16)


BF = jnp.bfloat16
F32 = jnp.float32
TILE = 16
FRAME = 168
DEAD = 256.0


def silu(values):
    half = 0.5 * values
    return half + half * jnp.tanh(half)


def mm(left, right):
    return jnp.dot(left, right, preferred_element_type=F32)


def iota(shape, dim):
    return lax.broadcasted_iota(jnp.int32, shape, dim)


def in_vmem():
    return pl.BlockSpec(memory_space=pltpu.VMEM)


def in_smem():
    return pl.BlockSpec(memory_space=pltpu.SMEM)


def in_any():
    return pl.BlockSpec(memory_space=pl.ANY)


def frame_kernel(me_ref, w_ref, val_ref, node_ref, count_ref, *refs):
    outs, (turned, slots, rows, frame) = refs[:4], refs[4:]
    me = me_ref[0]
    breadth, n_slots = val_ref.shape
    senders = count_ref.shape[1]
    capacity = n_slots // senders
    phase = lax.rem(WROWS * me, TILE)
    for r in range(WROWS):
        frame[pl.ds(phase + r, 1), :] = w_ref[0:1, D * r : D * (r + 1)].astype(F32)
    own = (iota((senders, n_slots), 0) == iota((senders, n_slots), 1) // capacity).astype(BF)
    counts = jnp.broadcast_to(count_ref[...], (8, senders)).astype(F32).astype(BF)
    live = mm(counts, own)[0:1, :]
    place = (iota((1, n_slots), 1) % capacity).astype(F32)
    code = jnp.where(place < live, node_ref[...].astype(F32) - DEAD, DEAD)
    turned[:breadth, :] = val_ref[...].astype(F32)
    line = iota((n_slots - breadth, n_slots), 0)
    tail = jnp.zeros((n_slots - breadth, n_slots), F32)
    for k in range(OBS_EDGES):
        tail = jnp.where(line == k, code[k : k + 1, :], tail)
    turned[breadth:, :] = tail
    slots[...] = turned[...].T
    for j in range(capacity):
        rows[:, 128 * j : 128 * (j + 1)] = slots[pl.ds(j, senders, stride=capacity), :]
    start = pl.multiple_of(jnp.where(phase >= 8, 0, FRAME - 8), 8)
    for flip in range(4):
        plane = (me >> 3) ^ flip
        frame[pl.ds(start, 8), :] = rows[pl.ds(pl.multiple_of(plane * 8, 8), 8), :]
        outs[flip][...] = frame[...].astype(BF)


def encoder_kernel(me_ref, *refs):
    pieces = refs[:16]
    init_ref, edge_ref, nbias_ref, gain_ref = refs[16:20]
    src_ref, tgt_ref, rest_ref, first_ref, pagg_ref, pout_ref = refs[20:26]
    big, heads, tails, obs, enc, proc = refs[26:]
    height = WROWS
    me = me_ref[0]
    core = me & 1
    for unit in range(4):
        for twin in range(2):
            ax = jnp.where((core ^ twin) == 0, 4, 2)
            ay = jnp.where((core ^ twin) == 0, 2, 4)
            for pair in range(2):
                for j in range(2):
                    piece = pieces[unit * 4 + twin * 2 + pair]
                    mask = (8 * unit) ^ twin ^ (ax if j else 0) ^ (ay if pair else 0)
                    dev = me ^ mask
                    row = pl.multiple_of((height * dev) // TILE * TILE + TILE, TILE)
                    heads[dev] = piece[j, 0:TILE, :]
                    big[pl.ds(row, 128), :] = piece[j, TILE : TILE + 128, :]
                    tails[dev, 0 : FRAME - 144, :] = piece[j, 144:FRAME, :]
    row16 = iota((TILE, D), 0)
    for dev in range(32):
        phase = height * dev % TILE
        tile = height * dev // TILE
        after = height * (dev + 1) // TILE
        head = heads[dev]
        if phase:
            before = height * (dev - 1) // TILE
            skip = TILE * (tile - before) - 144
            last = tails[dev - 1, skip : skip + TILE, :]
            head = jnp.where(row16 < phase, last.astype(F32), head.astype(F32)).astype(BF)
        big[TILE * tile : TILE * (tile + 1), :] = head
        if after - tile == 10:
            big[TILE * (tile + 9) : TILE * (tile + 10), :] = tails[dev, 0:TILE, :]
        if phase >= 8:
            seen = heads[dev].astype(F32)[0:8]
        else:
            seen = tails[dev, TILE : 2 * TILE, :].astype(F32)[0:8]
        for j in range(4):
            obs[j, 8 * dev : 8 * (dev + 1), :] = seen[:, 128 * j : 128 * (j + 1)]
    e0 = CH
    a0 = CH + 2 * D
    o0 = CH + 3 * D
    p0 = CH + 4 * D
    g0 = CH + 7 * D
    u0 = CH + 8 * D
    pagg_ref[...] = big[g0 : g0 + D, :]
    pout_ref[...] = big[u0 : u0 + D, :]
    out = iota((256, 256), 0)
    two = (iota((256, 256), 1) == 2 * (out & 127) + (out >> 7)).astype(BF)
    for j in range(D // 128):
        got = mm(two, big[e0 + 256 * j : e0 + 256 * (j + 1), :]).astype(BF)
        enc[0, 128 * j : 128 * (j + 1), :] = got[:128]
        enc[1, 128 * j : 128 * (j + 1), :] = got[128:]
    out = iota((384, 384), 0)
    three = (iota((384, 384), 1) == 3 * (out & 127) + (out >> 7)).astype(BF)
    for j in range(D // 128):
        got = mm(three, big[p0 + 384 * j : p0 + 384 * (j + 1), :]).astype(BF)
        for m in range(3):
            proc[m, 128 * j : 128 * (j + 1), :] = got[128 * m : 128 * (m + 1)]
    init = init_ref[...]
    query = mm(init, enc[0]) + edge_ref[0:1, :]
    slots = jnp.concatenate([obs[j, pl.ds(me & 7, 32, stride=8), :] for j in range(4)], axis=0)
    embedded = mm(slots[:, :CH].astype(BF), big[0:CH, :]).astype(BF).astype(F32)
    node_ids = iota((slots.shape[0], init.shape[0]), 1)
    picks = []
    for k in range(OBS_EDGES):
        code = slots[:, CH + k : CH + k + 1] + DEAD
        picks.append((node_ids == code.astype(jnp.int32)).astype(F32))
    select = jnp.concatenate(picks, axis=0)
    spread = select.astype(BF)
    q_high = query.astype(BF)
    q_low = (query - q_high.astype(F32)).astype(BF)
    picked = mm(spread, q_high) + mm(spread, q_low)
    message = silu(jnp.concatenate([embedded] * OBS_EDGES, axis=0) + picked)
    collect = select.T.astype(BF)
    m_high = message.astype(BF)
    m_low = (message - m_high.astype(F32)).astype(BF)
    gathered = (mm(collect, m_high) + mm(collect, m_low)).astype(BF)
    hidden = silu(
        mm(init, enc[1]) + mm(gathered, big[a0 : a0 + D, :]) + nbias_ref[0:1, :]
    ).astype(BF)
    first = (
        init.astype(F32) + layer_norm(mm(hidden, big[o0 : o0 + D, :]), gain_ref[0:1, :])
    ).astype(BF)
    first_ref[...] = first
    src_ref[...] = mm(first, proc[0]).astype(BF)
    tgt_ref[...] = mm(first, proc[1]) + edge_ref[1:2, :]
    rest_ref[...] = mm(first, proc[2]) + nbias_ref[1:2, :]


def processor_kernel(
    low_ref, src_ref, high_ref, tgt_ref, rest_ref, first_ref, off_ref, pagg_ref, pout_ref, gain_ref, out_ref, ext
):
    count = src_ref.shape[0]
    ext[0:HALO, :] = low_ref[...]
    ext[HALO : HALO + count, :] = src_ref[...]
    ext[HALO + count :, :] = high_ref[...]
    target = tgt_ref[...]
    cols = iota((count, count + 2 * HALO), 1) - iota((count, count + 2 * HALO), 0) - HALO
    pooled = jnp.zeros((count, D), F32)
    for k in range(DEG):
        select = (cols == off_ref[:, k : k + 1]).astype(BF)
        pooled = pooled + silu(mm(select, ext[...]) + target)
    hidden = silu(rest_ref[...] + mm(pooled.astype(BF), pagg_ref[...])).astype(BF)
    out_ref[...] = (
        first_ref[...].astype(F32) + layer_norm(mm(hidden, pout_ref[...]), gain_ref[1:2, :])
    ).astype(BF)


WROWS = 147


def fits(obs_values, obs_node, mesh_init, weights_flat):
    return (
        lax.axis_size("patch") == 8
        and lax.axis_size("lat") == 4
        and weights_flat.shape[1] == WROWS * D
        and obs_values.shape == (128, CH)
        and mesh_init.shape[0] <= 320
        and mesh_init.shape[0] >= HALO
    )


def spread_weights(frames):
    axes = ("patch", "lat")

    def move(block, masks):
        return lax.ppermute(block, axes, [(i, i ^ masks[i & 1]) for i in range(32)])

    units = [frames[0]] + [move(frames[f], (8 * f, 8 * f)) for f in (1, 2, 3)]
    pieces = []
    for unit in units:
        pair = jnp.stack([unit, move(unit, (4, 2))])
        other = move(pair, (2, 4))
        pieces += [pair, other, move(pair, (1, 1)), move(other, (1, 1))]
    return pieces


def shards(
    obs_values,
    obs_count,
    obs_node,
    mesh_init,
    mesh_offset,
    weights_flat,
    edge_bias,
    node_bias,
    norm_gain,
):
    if not fits(obs_values, obs_node, mesh_init, weights_flat):
        return general(
            obs_values,
            obs_count,
            obs_node,
            mesh_init,
            mesh_offset,
            weights_flat,
            edge_bias,
            node_bias,
            norm_gain,
        )
    axes = ("patch", "lat")
    me = lax.axis_index(axes).astype(jnp.int32).reshape(1)
    count = mesh_init.shape[0]
    frames = pl.pallas_call(
        frame_kernel,
        out_shape=[jax.ShapeDtypeStruct((FRAME, D), BF)] * 4,
        in_specs=[in_smem()] + [in_vmem()] * 4,
        out_specs=[in_vmem()] * 4,
        scratch_shapes=[
            pltpu.VMEM((128, 128), F32),
            pltpu.VMEM((128, 128), F32),
            pltpu.VMEM((32, D), F32),
            pltpu.VMEM((FRAME, D), F32),
        ],
        compiler_params=pltpu.CompilerParams(vmem_limit_bytes=8 << 20),
        name="frames",
    )(me, weights_flat, obs_values.T, obs_node.T, obs_count)
    pieces = spread_weights(frames)
    wide = jax.ShapeDtypeStruct((count, D), F32)
    slim = jax.ShapeDtypeStruct((count, D), BF)
    square = jax.ShapeDtypeStruct((D, D), BF)
    sources, target, rest, first, w_pagg, w_pout = pl.pallas_call(
        encoder_kernel,
        out_shape=[slim, wide, wide, slim, square, square],
        in_specs=[in_smem()] + [in_vmem()] * 16 + [in_vmem()] * 4,
        out_specs=[in_vmem()] * 6,
        scratch_shapes=[
            pltpu.VMEM((32 * WROWS, D), BF),
            pltpu.VMEM((32, TILE, D), BF),
            pltpu.VMEM((32, 2 * TILE, D), BF),
            pltpu.VMEM((4, 256, 128), F32),
            pltpu.VMEM((2, D, D), BF),
            pltpu.VMEM((3, D, D), BF),
        ],
        compiler_params=pltpu.CompilerParams(vmem_limit_bytes=34 << 20),
        name="encoder",
    )(me, *pieces, mesh_init, edge_bias, node_bias, norm_gain)
    forward = [(i, (i + 1) % 32) for i in range(32)]
    backward = [(j, i) for i, j in forward]
    low = lax.ppermute(sources[count - HALO :], axes, forward)
    high = lax.ppermute(sources[:HALO], axes, backward)
    return pl.pallas_call(
        processor_kernel,
        out_shape=slim,
        in_specs=[in_vmem()] * 10,
        out_specs=in_vmem(),
        scratch_shapes=[pltpu.VMEM((count + 2 * HALO, D), BF)],
        compiler_params=pltpu.CompilerParams(vmem_limit_bytes=20 << 20),
        name="processor",
    )(low, sources, high, target, rest, first, mesh_offset, w_pagg, w_pout, norm_gain)


def solution(mesh):
    return jax.shard_map(
        shards,
        mesh=mesh,
        in_specs=(
            P(("patch", "lat"), None),
            P(("patch", "lat"), None),
            P(("patch", "lat"), None),
            P(("patch", "lat"), None),
            P(("patch", "lat"), None),
            P(("patch", "lat"), None),
            P(),
            P(),
            P(),
        ),
        out_specs=P(("patch", "lat"), None),
        check_vma=False,
    )
```

```python
import jax
import jax.numpy as jnp
from jax import lax
from jax.experimental import pallas as pl
from jax.experimental.pallas import tpu as pltpu
from jax.sharding import PartitionSpec as P

D = 512
CH = 96
OBS_EDGES = 3
DEG = 6
HALO = 128


def extended(block, sides, width):
    for axis, dim in sides:
        count = lax.axis_size(axis)
        forward = [(i, i + 1) for i in range(count - 1)]
        forward.append((count - 1, 0))
        backward = [(target, source) for source, target in forward]
        low = lax.ppermute(
            lax.slice_in_dim(block, block.shape[dim] - width, None, axis=dim), axis, forward
        )
        high = lax.ppermute(lax.slice_in_dim(block, 0, width, axis=dim), axis, backward)
        block = jnp.concatenate([low, block, high], axis=dim)
    return block


def unpack(flat):
    shapes = ((CH, D), (D, 2 * D), (D, D), (D, D), (D, 3 * D), (D, D), (D, D))
    pieces = []
    offset = 0
    for height, breadth in shapes:
        pieces.append(flat[offset : offset + height * breadth].reshape(height, breadth))
        offset = offset + height * breadth
    return pieces


def layer_norm(values, gain):
    center = values - jnp.mean(values, axis=-1, keepdims=True)
    spread = jnp.mean(center * center, axis=-1, keepdims=True)
    return center * lax.rsqrt(spread + 1e-05) * gain


def embed_rows(rows, w_in):
    return jnp.dot(rows, w_in, preferred_element_type=jnp.float32).astype(jnp.bfloat16)


def deliver(values, nodes, counts):
    return (
        lax.all_to_all(
            lax.all_to_all(values, "patch", split_axis=0, concat_axis=0, tiled=True),
            "lat",
            split_axis=1,
            concat_axis=1,
            tiled=True,
        ),
        lax.all_to_all(
            lax.all_to_all(nodes, "patch", split_axis=0, concat_axis=0, tiled=True),
            "lat",
            split_axis=1,
            concat_axis=1,
            tiled=True,
        ),
        lax.all_to_all(
            lax.all_to_all(counts, "patch", split_axis=0, concat_axis=0, tiled=True),
            "lat",
            split_axis=1,
            concat_axis=1,
            tiled=True,
        ),
    )


def general(
    obs_values,
    obs_count,
    obs_node,
    mesh_init,
    mesh_offset,
    weights_flat,
    edge_bias,
    node_bias,
    norm_gain,
):
    n_patch = lax.axis_size("patch")
    n_lat = lax.axis_size("lat")
    senders = n_patch * n_lat
    capacity = obs_values.shape[0] // senders
    node_dev = mesh_init.shape[0]
    table = lax.all_gather(weights_flat, ("patch", "lat"), axis=0, tiled=True)
    w_in, w_enc, w_agg, w_out, w_proc, w_pagg, w_pout = unpack(table.reshape(-1))
    breadth = obs_values.shape[1]
    arrived, targets, counts = deliver(
        obs_values.reshape(n_patch, n_lat, capacity, breadth),
        obs_node.reshape(n_patch, n_lat, capacity, OBS_EDGES),
        obs_count.reshape(n_patch, n_lat),
    )
    arrived = arrived.reshape(senders * capacity, breadth)
    targets = targets.reshape(senders * capacity, OBS_EDGES)
    embedded = embed_rows(arrived, w_in)
    alive = (
        (jnp.arange(capacity, dtype=jnp.int32)[None, :] < counts.reshape(senders, 1))
        .astype(jnp.float32)
        .reshape(-1)
    )
    encoded = jnp.dot(mesh_init, w_enc, preferred_element_type=jnp.float32)
    query = encoded[:, :D] + edge_bias[0]
    total_rows = senders * capacity
    block = min(512, total_rows)
    turns = total_rows // block
    node_ids = jnp.arange(node_dev, dtype=jnp.int32)[None, :]

    def encode_block(block_index, totals):
        start = block_index * block
        piece = lax.dynamic_slice_in_dim(embedded, start, block, 0).astype(jnp.float32)
        nodes = lax.dynamic_slice_in_dim(targets, start, block, 0)
        weight = lax.dynamic_slice_in_dim(alive, start, block, 0)[:, None]
        for which in range(OBS_EDGES):
            selector = (nodes[:, which][:, None] == node_ids).astype(jnp.float32)
            picked = jnp.dot(selector, query, precision=lax.Precision.HIGHEST)
            message = jax.nn.silu(piece + picked) * weight
            totals = totals + lax.dot_general(
                selector, message, (((0,), (0,)), ((), ())), precision=lax.Precision.HIGHEST
            )
        return totals

    totals = lax.fori_loop(0, turns, encode_block, jnp.zeros((node_dev, D), jnp.float32))
    gathered = totals.astype(jnp.bfloat16)
    hidden = jax.nn.silu(
        encoded[:, D:] + jnp.dot(gathered, w_agg, preferred_element_type=jnp.float32) + node_bias[0]
    ).astype(jnp.bfloat16)
    first = (
        mesh_init.astype(jnp.float32)
        + layer_norm(jnp.dot(hidden, w_out, preferred_element_type=jnp.float32), norm_gain[0])
    ).astype(jnp.bfloat16)
    projected = jnp.dot(first, w_proc, preferred_element_type=jnp.float32)
    sources = projected[:, :D].astype(jnp.bfloat16)
    target = projected[:, D : 2 * D] + edge_bias[1]
    padded = extended(sources, ((("patch", "lat"), 0),), HALO)
    local_ids = jnp.arange(node_dev, dtype=jnp.int32) + HALO
    pooled = jnp.zeros((node_dev, D), jnp.float32)
    for which in range(DEG):
        anchor = local_ids + mesh_offset[:, which]
        pooled = pooled + jax.nn.silu(jnp.take(padded, anchor, axis=0).astype(jnp.float32) + target)
    hidden2 = jax.nn.silu(
        projected[:, 2 * D :]
        + jnp.dot(pooled.astype(jnp.bfloat16), w_pagg, preferred_element_type=jnp.float32)
        + node_bias[1]
    ).astype(jnp.bfloat16)
    return (
        first.astype(jnp.float32)
        + layer_norm(jnp.dot(hidden2, w_pout, preferred_element_type=jnp.float32), norm_gain[1])
    ).astype(jnp.bfloat16)


BF = jnp.bfloat16
F32 = jnp.float32
TILE = 16
FRAME = 176
DEAD = 256.0


def silu(values):
    half = 0.5 * values
    return half + half * jnp.tanh(half)


def mm(left, right):
    return jnp.dot(left, right, preferred_element_type=F32)


def iota(shape, dim):
    return lax.broadcasted_iota(jnp.int32, shape, dim)


def in_vmem():
    return pl.BlockSpec(memory_space=pltpu.VMEM)


def in_smem():
    return pl.BlockSpec(memory_space=pltpu.SMEM)


def frame_kernel(me_ref, w_ref, val_ref, node_ref, count_ref, *refs):
    outs, (turned, slots, rows, frame) = refs[:2], refs[2:]
    me = me_ref[0]
    breadth, n_slots = val_ref.shape
    senders = count_ref.shape[1]
    capacity = n_slots // senders
    phase = lax.rem(WROWS * me, TILE)
    for r in range(WROWS):
        frame[pl.ds(phase + r, 1), :] = w_ref[0:1, D * r : D * (r + 1)].astype(F32)
    own = (iota((senders, n_slots), 0) == iota((senders, n_slots), 1) // capacity).astype(BF)
    counts = jnp.broadcast_to(count_ref[...], (8, senders)).astype(F32).astype(BF)
    live = mm(counts, own)[0:1, :]
    place = (iota((1, n_slots), 1) % capacity).astype(F32)
    code = jnp.where(place < live, node_ref[...].astype(F32) - DEAD, DEAD)
    turned[:breadth, :] = val_ref[...].astype(F32)
    line = iota((n_slots - breadth, n_slots), 0)
    tail = jnp.zeros((n_slots - breadth, n_slots), F32)
    for k in range(OBS_EDGES):
        tail = jnp.where(line == k, code[k : k + 1, :], tail)
    turned[breadth:, :] = tail
    slots[...] = turned[...].T
    for j in range(capacity):
        rows[:, 128 * j : 128 * (j + 1)] = slots[pl.ds(j, senders, stride=capacity), :]
    start = pl.multiple_of(jnp.where(phase >= 8, 0, FRAME - 16), 8)
    for flip in range(2):
        for ref, spot, plane in (
            (frame, start, (me >> 3) ^ (2 * flip)),
            (frame, FRAME - 8, (me >> 3) ^ (2 * flip + 1)),
        ):
            ref[pl.ds(spot, 8), :] = rows[pl.ds(pl.multiple_of(plane * 8, 8), 8), :]
        outs[flip][...] = frame[...].astype(BF)


def encoder_kernel(me_ref, *refs):
    pieces = refs[:16]
    init_ref, edge_ref, nbias_ref, gain_ref = refs[16:20]
    src_ref, start_ref, end_ref, tgt_ref, rest_ref, first_ref, pagg_ref, pout_ref = refs[20:28]
    big, edges, obs, enc, proc = refs[28:]
    height = WROWS
    me = me_ref[0]
    core = me & 1
    for unit in range(4):
        for twin in range(2):
            ax = jnp.where((core ^ twin) == 0, 4, 2)
            ay = jnp.where((core ^ twin) == 0, 2, 4)
            for pair in range(2):
                for j in range(2):
                    piece = pieces[unit * 4 + twin * 2 + pair]
                    mask = (8 * unit) ^ twin ^ (ax if j else 0) ^ (ay if pair else 0)
                    dev = me ^ mask
                    row = pl.multiple_of((height * dev) // TILE * TILE + TILE, TILE)
                    edges[dev, 0:TILE, :] = piece[j, 0:TILE, :]
                    big[pl.ds(row, 128), :] = piece[j, TILE : TILE + 128, :]
                    edges[dev, TILE : 3 * TILE, :] = piece[j, 144:FRAME, :]
                    if unit % 2:
                        spot = jnp.where(lax.rem(height * dev, TILE) >= 8, 0, 32)
                        edges[dev, pl.ds(pl.multiple_of(spot, TILE), 8), :] = piece[j, FRAME - 8 :, :]
    row16 = iota((TILE, D), 0)
    for dev in range(32):
        phase = height * dev % TILE
        tile = height * dev // TILE
        after = height * (dev + 1) // TILE
        head = edges[dev, 0:TILE, :]
        if phase:
            before = height * (dev - 1) // TILE
            skip = TILE * (tile - before) - 144
            last = edges[dev - 1, TILE + skip : 2 * TILE + skip, :]
            head = jnp.where(row16 < phase, last.astype(F32), head.astype(F32)).astype(BF)
        big[TILE * tile : TILE * (tile + 1), :] = head
        if after - tile == 10:
            big[TILE * (tile + 9) : TILE * (tile + 10), :] = edges[dev, TILE : 2 * TILE, :]
        if phase >= 8:
            seen = edges[dev, 0:TILE, :].astype(F32)[0:8]
        else:
            seen = edges[dev, 2 * TILE : 3 * TILE, :].astype(F32)[0:8]
        for j in range(4):
            obs[j, 8 * dev : 8 * (dev + 1), :] = seen[:, 128 * j : 128 * (j + 1)]
    e0 = CH
    a0 = CH + 2 * D
    o0 = CH + 3 * D
    p0 = CH + 4 * D
    g0 = CH + 7 * D
    u0 = CH + 8 * D
    pagg_ref[...] = big[g0 : g0 + D, :]
    pout_ref[...] = big[u0 : u0 + D, :]
    out = iota((256, 256), 0)
    two = (iota((256, 256), 1) == 2 * (out & 127) + (out >> 7)).astype(BF)
    for j in range(D // 128):
        got = mm(two, big[e0 + 256 * j : e0 + 256 * (j + 1), :]).astype(BF)
        enc[0, 128 * j : 128 * (j + 1), :] = got[:128]
        enc[1, 128 * j : 128 * (j + 1), :] = got[128:]
    out = iota((384, 384), 0)
    three = (iota((384, 384), 1) == 3 * (out & 127) + (out >> 7)).astype(BF)
    for j in range(D // 128):
        got = mm(three, big[p0 + 384 * j : p0 + 384 * (j + 1), :]).astype(BF)
        for m in range(3):
            proc[m, 128 * j : 128 * (j + 1), :] = got[128 * m : 128 * (m + 1)]
    init = init_ref[...]
    query = mm(init, enc[0]) + edge_ref[0:1, :]
    slots = jnp.concatenate([obs[j, pl.ds(me & 7, 32, stride=8), :] for j in range(4)], axis=0)
    embedded = mm(slots[:, :CH].astype(BF), big[0:CH, :]).astype(BF).astype(F32)
    node_ids = iota((slots.shape[0], init.shape[0]), 1)
    picks = []
    for k in range(OBS_EDGES):
        code = slots[:, CH + k : CH + k + 1] + DEAD
        picks.append((node_ids == code.astype(jnp.int32)).astype(F32))
    select = jnp.concatenate(picks, axis=0)
    spread = select.astype(BF)
    q_high = query.astype(BF)
    q_low = (query - q_high.astype(F32)).astype(BF)
    picked = mm(spread, q_high) + mm(spread, q_low)
    message = silu(jnp.concatenate([embedded] * OBS_EDGES, axis=0) + picked)
    collect = select.T.astype(BF)
    m_high = message.astype(BF)
    m_low = (message - m_high.astype(F32)).astype(BF)
    gathered = (mm(collect, m_high) + mm(collect, m_low)).astype(BF)
    hidden = silu(
        mm(init, enc[1]) + mm(gathered, big[a0 : a0 + D, :]) + nbias_ref[0:1, :]
    ).astype(BF)
    first = (
        init.astype(F32) + layer_norm(mm(hidden, big[o0 : o0 + D, :]), gain_ref[0:1, :])
    ).astype(BF)
    first_ref[...] = first
    sources = mm(first, proc[0]).astype(BF)
    src_ref[...] = sources
    start_ref[...] = sources[:HALO]
    end_ref[...] = sources[sources.shape[0] - HALO :]
    tgt_ref[...] = mm(first, proc[1]) + edge_ref[1:2, :]
    rest_ref[...] = mm(first, proc[2]) + nbias_ref[1:2, :]


def processor_kernel(
    low_ref, src_ref, high_ref, tgt_ref, rest_ref, first_ref, off_ref, pagg_ref, pout_ref, gain_ref, out_ref, ext
):
    count = src_ref.shape[0]
    ext[0:HALO, :] = low_ref[...]
    ext[HALO : HALO + count, :] = src_ref[...]
    ext[HALO + count :, :] = high_ref[...]
    block = count // 2
    span = block + 2 * HALO
    cols = iota((block, span), 1) - iota((block, span), 0) - HALO
    sums = []
    for at in range(0, count, block):
        select = jnp.concatenate(
            [(cols == off_ref[at : at + block, k : k + 1]).astype(F32) for k in range(DEG)], axis=0
        ).astype(BF)
        picked = mm(select, ext[at : at + span, :])
        target = tgt_ref[at : at + block, :]
        total = silu(picked[:block] + target)
        for k in range(1, DEG):
            total = total + silu(picked[block * k : block * (k + 1)] + target)
        sums.append(total)
    pooled = jnp.concatenate(sums, axis=0)
    hidden = silu(rest_ref[...] + mm(pooled.astype(BF), pagg_ref[...])).astype(BF)
    out_ref[...] = (
        first_ref[...].astype(F32) + layer_norm(mm(hidden, pout_ref[...]), gain_ref[1:2, :])
    ).astype(BF)


WROWS = 147


def fits(obs_values, mesh_init, weights_flat):
    return (
        lax.axis_size("patch") == 8
        and lax.axis_size("lat") == 4
        and weights_flat.shape[1] == WROWS * D
        and obs_values.shape == (128, CH)
        and mesh_init.shape[0] <= 320
        and mesh_init.shape[0] >= HALO
        and mesh_init.shape[0] % 32 == 0
    )


def spread_weights(near, far):
    axes = ("patch", "lat")

    def move(block, masks):
        return lax.ppermute(block, axes, [(i, i ^ masks[i & 1]) for i in range(32)])

    beside = move(near, (4, 2))
    opposite = move(far, (16, 16))
    aside = move(opposite, (4, 2))
    pieces = []
    for unit, twin in (
        (near, beside),
        (move(near, (8, 8)), move(beside, (8, 8))),
        (opposite, aside),
        (move(opposite, (8, 8)), move(aside, (8, 8))),
    ):
        pair = jnp.stack([unit, twin])
        other = move(pair, (2, 4))
        pieces += [pair, other, move(pair, (1, 1)), move(other, (1, 1))]
    return pieces


def shards(
    obs_values,
    obs_count,
    obs_node,
    mesh_init,
    mesh_offset,
    weights_flat,
    edge_bias,
    node_bias,
    norm_gain,
):
    if not fits(obs_values, mesh_init, weights_flat):
        return general(
            obs_values,
            obs_count,
            obs_node,
            mesh_init,
            mesh_offset,
            weights_flat,
            edge_bias,
            node_bias,
            norm_gain,
        )
    axes = ("patch", "lat")
    me = lax.axis_index(axes).astype(jnp.int32).reshape(1)
    count = mesh_init.shape[0]
    frames = pl.pallas_call(
        frame_kernel,
        out_shape=[jax.ShapeDtypeStruct((FRAME, D), BF)] * 2,
        in_specs=[in_smem()] + [in_vmem()] * 4,
        out_specs=[in_vmem()] * 2,
        scratch_shapes=[
            pltpu.VMEM((128, 128), F32),
            pltpu.VMEM((128, 128), F32),
            pltpu.VMEM((32, D), F32),
            pltpu.VMEM((FRAME, D), F32),
        ],
        compiler_params=pltpu.CompilerParams(vmem_limit_bytes=8 << 20),
        name="frames",
    )(me, weights_flat, obs_values.T, obs_node.T, obs_count)
    pieces = spread_weights(*frames)
    wide = jax.ShapeDtypeStruct((count, D), F32)
    slim = jax.ShapeDtypeStruct((count, D), BF)
    square = jax.ShapeDtypeStruct((D, D), BF)
    side = jax.ShapeDtypeStruct((HALO, D), BF)
    sources, start, end, target, rest, first, w_pagg, w_pout = pl.pallas_call(
        encoder_kernel,
        out_shape=[slim, side, side, wide, wide, slim, square, square],
        in_specs=[in_smem()] + [in_vmem()] * 16 + [in_vmem()] * 4,
        out_specs=[in_vmem()] * 8,
        scratch_shapes=[
            pltpu.VMEM((32 * WROWS, D), BF),
            pltpu.VMEM((32, 3 * TILE, D), BF),
            pltpu.VMEM((4, 256, 128), F32),
            pltpu.VMEM((2, D, D), BF),
            pltpu.VMEM((3, D, D), BF),
        ],
        compiler_params=pltpu.CompilerParams(vmem_limit_bytes=34 << 20),
        name="encoder",
    )(me, *pieces, mesh_init, edge_bias, node_bias, norm_gain)
    forward = [(i, (i + 1) % 32) for i in range(32)]
    backward = [(j, i) for i, j in forward]
    low = lax.ppermute(end, axes, forward)
    high = lax.ppermute(start, axes, backward)
    return pl.pallas_call(
        processor_kernel,
        out_shape=slim,
        in_specs=[in_vmem()] * 10,
        out_specs=in_vmem(),
        scratch_shapes=[pltpu.VMEM((count + 2 * HALO, D), BF)],
        compiler_params=pltpu.CompilerParams(vmem_limit_bytes=20 << 20),
        name="processor",
    )(low, sources, high, target, rest, first, mesh_offset, w_pagg, w_pout, norm_gain)


def solution(mesh):
    return jax.shard_map(
        shards,
        mesh=mesh,
        in_specs=(
            P(("patch", "lat"), None),
            P(("patch", "lat"), None),
            P(("patch", "lat"), None),
            P(("patch", "lat"), None),
            P(("patch", "lat"), None),
            P(("patch", "lat"), None),
            P(),
            P(),
            P(),
        ),
        out_specs=P(("patch", "lat"), None),
        check_vma=False,
    )
```

```python
import jax
import jax.numpy as jnp
from jax import lax
from jax.experimental import pallas as pl
from jax.experimental.pallas import tpu as pltpu
from jax.sharding import PartitionSpec as P

D = 512
CH = 96
OBS_EDGES = 3
DEG = 6
HALO = 128


def extended(block, sides, width):
    for axis, dim in sides:
        count = lax.axis_size(axis)
        forward = [(i, i + 1) for i in range(count - 1)]
        forward.append((count - 1, 0))
        backward = [(target, source) for source, target in forward]
        low = lax.ppermute(
            lax.slice_in_dim(block, block.shape[dim] - width, None, axis=dim), axis, forward
        )
        high = lax.ppermute(lax.slice_in_dim(block, 0, width, axis=dim), axis, backward)
        block = jnp.concatenate([low, block, high], axis=dim)
    return block


def unpack(flat):
    shapes = ((CH, D), (D, 2 * D), (D, D), (D, D), (D, 3 * D), (D, D), (D, D))
    pieces = []
    offset = 0
    for height, breadth in shapes:
        pieces.append(flat[offset : offset + height * breadth].reshape(height, breadth))
        offset = offset + height * breadth
    return pieces


def layer_norm(values, gain):
    center = values - jnp.mean(values, axis=-1, keepdims=True)
    spread = jnp.mean(center * center, axis=-1, keepdims=True)
    return center * lax.rsqrt(spread + 1e-05) * gain


def embed_rows(rows, w_in):
    return jnp.dot(rows, w_in, preferred_element_type=jnp.float32).astype(jnp.bfloat16)


def deliver(values, nodes, counts):
    return (
        lax.all_to_all(
            lax.all_to_all(values, "patch", split_axis=0, concat_axis=0, tiled=True),
            "lat",
            split_axis=1,
            concat_axis=1,
            tiled=True,
        ),
        lax.all_to_all(
            lax.all_to_all(nodes, "patch", split_axis=0, concat_axis=0, tiled=True),
            "lat",
            split_axis=1,
            concat_axis=1,
            tiled=True,
        ),
        lax.all_to_all(
            lax.all_to_all(counts, "patch", split_axis=0, concat_axis=0, tiled=True),
            "lat",
            split_axis=1,
            concat_axis=1,
            tiled=True,
        ),
    )


def general(
    obs_values,
    obs_count,
    obs_node,
    mesh_init,
    mesh_offset,
    weights_flat,
    edge_bias,
    node_bias,
    norm_gain,
):
    n_patch = lax.axis_size("patch")
    n_lat = lax.axis_size("lat")
    senders = n_patch * n_lat
    capacity = obs_values.shape[0] // senders
    node_dev = mesh_init.shape[0]
    table = lax.all_gather(weights_flat, ("patch", "lat"), axis=0, tiled=True)
    w_in, w_enc, w_agg, w_out, w_proc, w_pagg, w_pout = unpack(table.reshape(-1))
    breadth = obs_values.shape[1]
    arrived, targets, counts = deliver(
        obs_values.reshape(n_patch, n_lat, capacity, breadth),
        obs_node.reshape(n_patch, n_lat, capacity, OBS_EDGES),
        obs_count.reshape(n_patch, n_lat),
    )
    arrived = arrived.reshape(senders * capacity, breadth)
    targets = targets.reshape(senders * capacity, OBS_EDGES)
    embedded = embed_rows(arrived, w_in)
    alive = (
        (jnp.arange(capacity, dtype=jnp.int32)[None, :] < counts.reshape(senders, 1))
        .astype(jnp.float32)
        .reshape(-1)
    )
    encoded = jnp.dot(mesh_init, w_enc, preferred_element_type=jnp.float32)
    query = encoded[:, :D] + edge_bias[0]
    total_rows = senders * capacity
    block = min(512, total_rows)
    turns = total_rows // block
    node_ids = jnp.arange(node_dev, dtype=jnp.int32)[None, :]

    def encode_block(block_index, totals):
        start = block_index * block
        piece = lax.dynamic_slice_in_dim(embedded, start, block, 0).astype(jnp.float32)
        nodes = lax.dynamic_slice_in_dim(targets, start, block, 0)
        weight = lax.dynamic_slice_in_dim(alive, start, block, 0)[:, None]
        for which in range(OBS_EDGES):
            selector = (nodes[:, which][:, None] == node_ids).astype(jnp.float32)
            picked = jnp.dot(selector, query, precision=lax.Precision.HIGHEST)
            message = jax.nn.silu(piece + picked) * weight
            totals = totals + lax.dot_general(
                selector, message, (((0,), (0,)), ((), ())), precision=lax.Precision.HIGHEST
            )
        return totals

    totals = lax.fori_loop(0, turns, encode_block, jnp.zeros((node_dev, D), jnp.float32))
    gathered = totals.astype(jnp.bfloat16)
    hidden = jax.nn.silu(
        encoded[:, D:] + jnp.dot(gathered, w_agg, preferred_element_type=jnp.float32) + node_bias[0]
    ).astype(jnp.bfloat16)
    first = (
        mesh_init.astype(jnp.float32)
        + layer_norm(jnp.dot(hidden, w_out, preferred_element_type=jnp.float32), norm_gain[0])
    ).astype(jnp.bfloat16)
    projected = jnp.dot(first, w_proc, preferred_element_type=jnp.float32)
    sources = projected[:, :D].astype(jnp.bfloat16)
    target = projected[:, D : 2 * D] + edge_bias[1]
    padded = extended(sources, ((("patch", "lat"), 0),), HALO)
    local_ids = jnp.arange(node_dev, dtype=jnp.int32) + HALO
    pooled = jnp.zeros((node_dev, D), jnp.float32)
    for which in range(DEG):
        anchor = local_ids + mesh_offset[:, which]
        pooled = pooled + jax.nn.silu(jnp.take(padded, anchor, axis=0).astype(jnp.float32) + target)
    hidden2 = jax.nn.silu(
        projected[:, 2 * D :]
        + jnp.dot(pooled.astype(jnp.bfloat16), w_pagg, preferred_element_type=jnp.float32)
        + node_bias[1]
    ).astype(jnp.bfloat16)
    return (
        first.astype(jnp.float32)
        + layer_norm(jnp.dot(hidden2, w_pout, preferred_element_type=jnp.float32), norm_gain[1])
    ).astype(jnp.bfloat16)


BF = jnp.bfloat16
F32 = jnp.float32
TILE = 16
FRAME = 176
DEAD = 256.0


def silu(values):
    half = 0.5 * values
    return half + half * jnp.tanh(half)


def mm(left, right):
    return jnp.dot(left, right, preferred_element_type=F32)


def iota(shape, dim):
    return lax.broadcasted_iota(jnp.int32, shape, dim)


def in_vmem():
    return pl.BlockSpec(memory_space=pltpu.VMEM)


def in_smem():
    return pl.BlockSpec(memory_space=pltpu.SMEM)


def in_any():
    return pl.BlockSpec(memory_space=pltpu.HBM)


def frame_kernel(me_ref, *refs):
    outs = refs[4:6]
    w_ref, val_ref, node_ref, count_ref, turned, slots, rows, frame, sems = refs[6:]
    copies = [
        pltpu.make_async_copy(src, dst, sems.at[i])
        for i, (src, dst) in enumerate(zip(refs[:4], (w_ref, val_ref, node_ref, count_ref)))
    ]
    for copy in copies:
        copy.start()
    for copy in copies:
        copy.wait()
    me = me_ref[0]
    breadth, n_slots = val_ref.shape
    senders = count_ref.shape[1]
    capacity = n_slots // senders
    phase = lax.rem(WROWS * me, TILE)
    for r in range(WROWS):
        frame[pl.ds(phase + r, 1), :] = w_ref[0:1, D * r : D * (r + 1)].astype(F32)
    own = (iota((senders, n_slots), 0) == iota((senders, n_slots), 1) // capacity).astype(BF)
    counts = jnp.broadcast_to(count_ref[...], (8, senders)).astype(F32).astype(BF)
    live = mm(counts, own)[0:1, :]
    place = (iota((1, n_slots), 1) % capacity).astype(F32)
    code = jnp.where(place < live, node_ref[...].astype(F32) - DEAD, DEAD)
    turned[:breadth, :] = val_ref[...].astype(F32)
    feature = iota((n_slots - breadth, n_slots), 0)
    tail = jnp.zeros((n_slots - breadth, n_slots), F32)
    for k in range(OBS_EDGES):
        tail = jnp.where(feature == k, code[k : k + 1, :], tail)
    turned[breadth:, :] = tail
    slots[...] = turned[...].T
    for j in range(capacity):
        rows[:, 128 * j : 128 * (j + 1)] = slots[pl.ds(j, senders, stride=capacity), :]
    start = pl.multiple_of(jnp.where(phase >= 8, 0, FRAME - 16), 8)
    lane = iota((8, 128), 1)
    line = iota((8, 128), 0)
    used = breadth + OBS_EDGES
    quarter = breadth // capacity

    def block(plane):
        before = slots[pl.ds(pl.multiple_of(lax.rem(32 * plane + 120, 128), 8), 8), :]
        after = slots[pl.ds(pl.multiple_of(lax.rem(32 * plane + 32, 128), 8), 8), :]
        extra = pltpu.roll(jnp.where(line < 4, after, before), 4, 0)
        base = rows[pl.ds(pl.multiple_of(8 * plane, 8), 8), :]
        parts = []
        for g in range(capacity):
            moved = pltpu.roll(extra, (used - quarter * g) % 128, 1)
            keep = (lane >= used) & (lane < used + quarter)
            parts.append(jnp.where(keep, moved, base[:, 128 * g : 128 * (g + 1)]))
        keep = (lane >= used + quarter) & (lane < used + quarter + OBS_EDGES)
        parts[0] = jnp.where(keep, pltpu.roll(extra, used + quarter - breadth, 1), parts[0])
        return jnp.concatenate(parts, axis=1)

    for flip in range(2):
        frame[pl.ds(start, 8), :] = block((me >> 3) ^ (2 * flip))
        frame[FRAME - 8 :, :] = block((me >> 3) ^ (2 * flip + 1))
        outs[flip][...] = frame[...].astype(BF)


def layer_kernel(me_ref, *refs):
    pieces = refs[:16]
    low_ref, init_ref, high_ref, off_ref, edge_ref, nbias_ref, gain_ref, out_ref = refs[16:24]
    big, edges, obs, enc, proc, ext, wide = refs[24:]
    count = init_ref.shape[0]
    height = WROWS
    me = me_ref[0]
    core = me & 1
    for unit in range(4):
        for twin in range(2):
            ax = jnp.where((core ^ twin) == 0, 4, 2)
            ay = jnp.where((core ^ twin) == 0, 2, 4)
            for pair in range(2):
                for j in range(2):
                    piece = pieces[unit * 4 + twin * 2 + pair]
                    mask = (8 * unit) ^ twin ^ (ax if j else 0) ^ (ay if pair else 0)
                    dev = me ^ mask
                    row = pl.multiple_of((height * dev) // TILE * TILE + TILE, TILE)
                    edges[dev, 0:TILE, :] = piece[j, 0:TILE, :]
                    big[pl.ds(row, 128), :] = piece[j, TILE : TILE + 128, :]
                    edges[dev, TILE : 3 * TILE, :] = piece[j, 144:FRAME, :]
                    if unit % 2:
                        spot = jnp.where(lax.rem(height * dev, TILE) >= 8, 0, 32)
                        edges[dev, pl.ds(pl.multiple_of(spot, TILE), 8), :] = piece[j, FRAME - 8 :, :]
    row16 = iota((TILE, D), 0)
    for dev in range(32):
        phase = height * dev % TILE
        tile = height * dev // TILE
        after = height * (dev + 1) // TILE
        head = edges[dev, 0:TILE, :]
        if phase:
            before = height * (dev - 1) // TILE
            skip = TILE * (tile - before) - 144
            last = edges[dev - 1, TILE + skip : 2 * TILE + skip, :]
            head = jnp.where(row16 < phase, last.astype(F32), head.astype(F32)).astype(BF)
        big[TILE * tile : TILE * (tile + 1), :] = head
        if after - tile == 10:
            big[TILE * (tile + 9) : TILE * (tile + 10), :] = edges[dev, TILE : 2 * TILE, :]
        if phase >= 8:
            seen = edges[dev, 0:TILE, :].astype(F32)[0:8]
        else:
            seen = edges[dev, 2 * TILE : 3 * TILE, :].astype(F32)[0:8]
        for j in range(4):
            obs[j, 8 * dev : 8 * (dev + 1), :] = seen[:, 128 * j : 128 * (j + 1)]
    e0 = CH
    a0 = CH + 2 * D
    o0 = CH + 3 * D
    p0 = CH + 4 * D
    g0 = CH + 7 * D
    u0 = CH + 8 * D
    for base, fold, dest in ((e0, 2, enc), (p0, 3, proc)):
        for j in range(4):
            lanes = slice(128 * j, 128 * (j + 1))
            wide[j, 0 : fold * D, :] = big[base : base + fold * D, lanes].astype(F32)
            for m in range(fold):
                dest[m, :, lanes] = wide[j, pl.ds(m, D, stride=fold), :].astype(BF)
    init = jnp.concatenate([low_ref[...], init_ref[...], high_ref[...]], axis=0)
    query = (mm(init, enc[0]) + edge_ref[0:1, :]).astype(BF)
    spot = me & 7
    lane = iota((32, 128), 1)
    used = CH + OBS_EDGES
    quarter = CH // 4

    def direct(row):
        return jnp.concatenate([obs[j, pl.ds(row, 32, stride=8), :] for j in range(4)], axis=0)

    def spilled(row):
        groups = []
        for j in range(4):
            near = obs[0, pl.ds(row + j, 32, stride=8), :]
            slot = pltpu.roll(near, (CH - used - quarter) % 128, 1)
            for g in range(4):
                part = near if g == 0 else obs[g, pl.ds(row + j, 32, stride=8), :]
                keep = (lane >= quarter * g) & (lane < quarter * (g + 1))
                slot = jnp.where(keep, pltpu.roll(part, (quarter * g - used) % 128, 1), slot)
            groups.append(slot)
        return jnp.concatenate(groups, axis=0)

    before = jnp.where(spot > 0, direct(jnp.maximum(spot - 1, 0)), spilled(0))
    after = jnp.where(spot < 7, direct(jnp.minimum(spot + 1, 7)), spilled(4))
    rows = [before, direct(spot), after]
    per = rows[0].shape[0]
    joined = jnp.concatenate(rows, axis=0)
    embedded = mm(joined[:, :CH].astype(BF), big[0:CH, :]).astype(BF).astype(F32)
    sums = []
    for part, shift, top, size in (
        (0, count - HALO, 0, HALO),
        (1, 0, HALO, count),
        (2, 0, HALO + count, HALO),
    ):
        slots = rows[part]
        embeds = embedded[per * part : per * (part + 1)]
        node_ids = iota((slots.shape[0], size), 1)
        picks = []
        for k in range(OBS_EDGES):
            code = slots[:, CH + k : CH + k + 1] + (DEAD - shift)
            picks.append((node_ids == code.astype(jnp.int32)).astype(F32))
        select = jnp.concatenate(picks, axis=0)
        picked = mm(select.astype(BF), query[top : top + size])
        message = silu(jnp.concatenate([embeds] * OBS_EDGES, axis=0) + picked)
        sums.append(mm(select.T.astype(BF), message.astype(BF)).astype(BF))
    gathered = jnp.concatenate(sums, axis=0)
    hidden = silu(
        mm(init, enc[1]) + mm(gathered, big[a0 : a0 + D, :]) + nbias_ref[0:1, :]
    ).astype(BF)
    first = (
        init.astype(F32) + layer_norm(mm(hidden, big[o0 : o0 + D, :]), gain_ref[0:1, :])
    ).astype(BF)
    ext[...] = mm(first, proc[0]).astype(BF)
    first = first[HALO : HALO + count]
    block = count // 2
    span = block + 2 * HALO
    cols = iota((block, span), 1) - iota((block, span), 0) - HALO
    target = mm(first, proc[1]) + edge_ref[1:2, :]
    sums = []
    for at in range(0, count, block):
        select = jnp.concatenate(
            [(cols == off_ref[at : at + block, k : k + 1]).astype(F32) for k in range(DEG)], axis=0
        ).astype(BF)
        picked = mm(select, ext[at : at + span, :])
        base = target[at : at + block]
        total = silu(picked[:block] + base)
        for k in range(1, DEG):
            total = total + silu(picked[block * k : block * (k + 1)] + base)
        sums.append(total)
    pooled = jnp.concatenate(sums, axis=0).astype(BF)
    hidden = silu(
        mm(first, proc[2]) + nbias_ref[1:2, :] + mm(pooled, big[g0 : g0 + D, :])
    ).astype(BF)
    out_ref[...] = (
        first.astype(F32) + layer_norm(mm(hidden, big[u0 : u0 + D, :]), gain_ref[1:2, :])
    ).astype(BF)


WROWS = 147


def fits(obs_values, mesh_init, weights_flat):
    return (
        lax.axis_size("patch") == 8
        and lax.axis_size("lat") == 4
        and weights_flat.shape[1] == WROWS * D
        and obs_values.shape == (128, CH)
        and mesh_init.shape[0] <= 320
        and mesh_init.shape[0] >= HALO
        and mesh_init.shape[0] % 32 == 0
    )


def spread_weights(near, far, init):
    axes = ("patch", "lat")
    count = init.shape[0]
    ring = [(i, (i + 1) % 32) for i in range(32)]

    def move(block, masks):
        return lax.ppermute(block, axes, [(i, i ^ masks[i & 1]) for i in range(32)])

    low = lax.ppermute(init[count - HALO :], axes, ring)
    high = lax.ppermute(init[:HALO], axes, [(j, i) for i, j in ring])
    beside = move(near, (4, 2))
    opposite = move(far, (16, 16))
    aside = move(opposite, (4, 2))
    pieces = []
    for unit, twin in (
        (near, beside),
        (move(near, (8, 8)), move(beside, (8, 8))),
        (opposite, aside),
        (move(opposite, (8, 8)), move(aside, (8, 8))),
    ):
        pair = jnp.stack([unit, twin])
        other = move(pair, (2, 4))
        pieces += [pair, other, move(pair, (1, 1)), move(other, (1, 1))]
    return pieces + [low, init, high]


def shards(
    obs_values,
    obs_count,
    obs_node,
    mesh_init,
    mesh_offset,
    weights_flat,
    edge_bias,
    node_bias,
    norm_gain,
):
    if not fits(obs_values, mesh_init, weights_flat):
        return general(
            obs_values,
            obs_count,
            obs_node,
            mesh_init,
            mesh_offset,
            weights_flat,
            edge_bias,
            node_bias,
            norm_gain,
        )
    axes = ("patch", "lat")
    me = lax.axis_index(axes).astype(jnp.int32).reshape(1)
    count = mesh_init.shape[0]
    frames = pl.pallas_call(
        frame_kernel,
        out_shape=[jax.ShapeDtypeStruct((FRAME, D), BF)] * 2,
        in_specs=[in_smem()] + [in_any()] * 4,
        out_specs=[in_vmem()] * 2,
        scratch_shapes=[
            pltpu.VMEM(weights_flat.shape, BF),
            pltpu.VMEM(obs_values.shape[::-1], BF),
            pltpu.VMEM(obs_node.shape[::-1], jnp.int32),
            pltpu.VMEM(obs_count.shape, jnp.int32),
            pltpu.VMEM((128, 128), F32),
            pltpu.VMEM((128, 128), F32),
            pltpu.VMEM((32, D), F32),
            pltpu.VMEM((FRAME, D), F32),
            pltpu.SemaphoreType.DMA((4,)),
        ],
        compiler_params=pltpu.CompilerParams(vmem_limit_bytes=60 << 20),
        name="frames",
    )(me, weights_flat, obs_values.T, obs_node.T, obs_count)
    pieces = spread_weights(*frames, mesh_init)
    return pl.pallas_call(
        layer_kernel,
        out_shape=jax.ShapeDtypeStruct((count, D), BF),
        in_specs=[in_smem()] + [in_vmem()] * 23,
        out_specs=in_vmem(),
        scratch_shapes=[
            pltpu.VMEM((32 * WROWS, D), BF),
            pltpu.VMEM((32, 3 * TILE, D), BF),
            pltpu.VMEM((4, 256, 128), F32),
            pltpu.VMEM((2, D, D), BF),
            pltpu.VMEM((3, D, D), BF),
            pltpu.VMEM((count + 2 * HALO, D), BF),
            pltpu.VMEM((4, 3 * D, 128), F32),
        ],
        compiler_params=pltpu.CompilerParams(vmem_limit_bytes=40 << 20),
        name="layer",
    )(me, *pieces, mesh_offset, edge_bias, node_bias, norm_gain)


def solution(mesh):
    return jax.shard_map(
        shards,
        mesh=mesh,
        in_specs=(
            P(("patch", "lat"), None),
            P(("patch", "lat"), None),
            P(("patch", "lat"), None),
            P(("patch", "lat"), None),
            P(("patch", "lat"), None),
            P(("patch", "lat"), None),
            P(),
            P(),
            P(),
        ),
        out_specs=P(("patch", "lat"), None),
        check_vma=False,
    )
```

```python
import jax
import jax.numpy as jnp
from jax import lax
from jax.experimental import pallas as pl
from jax.experimental.pallas import tpu as pltpu
from jax.sharding import PartitionSpec as P

D = 512
CH = 96
OBS_EDGES = 3
DEG = 6
HALO = 128


def extended(block, sides, width):
    for axis, dim in sides:
        count = lax.axis_size(axis)
        forward = [(i, i + 1) for i in range(count - 1)]
        forward.append((count - 1, 0))
        backward = [(target, source) for source, target in forward]
        low = lax.ppermute(
            lax.slice_in_dim(block, block.shape[dim] - width, None, axis=dim), axis, forward
        )
        high = lax.ppermute(lax.slice_in_dim(block, 0, width, axis=dim), axis, backward)
        block = jnp.concatenate([low, block, high], axis=dim)
    return block


def unpack(flat):
    shapes = ((CH, D), (D, 2 * D), (D, D), (D, D), (D, 3 * D), (D, D), (D, D))
    pieces = []
    offset = 0
    for height, breadth in shapes:
        pieces.append(flat[offset : offset + height * breadth].reshape(height, breadth))
        offset = offset + height * breadth
    return pieces


def layer_norm(values, gain):
    center = values - jnp.mean(values, axis=-1, keepdims=True)
    spread = jnp.mean(center * center, axis=-1, keepdims=True)
    return center * lax.rsqrt(spread + 1e-05) * gain


def embed_rows(rows, w_in):
    return jnp.dot(rows, w_in, preferred_element_type=jnp.float32).astype(jnp.bfloat16)


def deliver(values, nodes, counts):
    return (
        lax.all_to_all(
            lax.all_to_all(values, "patch", split_axis=0, concat_axis=0, tiled=True),
            "lat",
            split_axis=1,
            concat_axis=1,
            tiled=True,
        ),
        lax.all_to_all(
            lax.all_to_all(nodes, "patch", split_axis=0, concat_axis=0, tiled=True),
            "lat",
            split_axis=1,
            concat_axis=1,
            tiled=True,
        ),
        lax.all_to_all(
            lax.all_to_all(counts, "patch", split_axis=0, concat_axis=0, tiled=True),
            "lat",
            split_axis=1,
            concat_axis=1,
            tiled=True,
        ),
    )


def general(
    obs_values,
    obs_count,
    obs_node,
    mesh_init,
    mesh_offset,
    weights_flat,
    edge_bias,
    node_bias,
    norm_gain,
):
    n_patch = lax.axis_size("patch")
    n_lat = lax.axis_size("lat")
    senders = n_patch * n_lat
    capacity = obs_values.shape[0] // senders
    node_dev = mesh_init.shape[0]
    table = lax.all_gather(weights_flat, ("patch", "lat"), axis=0, tiled=True)
    w_in, w_enc, w_agg, w_out, w_proc, w_pagg, w_pout = unpack(table.reshape(-1))
    breadth = obs_values.shape[1]
    arrived, targets, counts = deliver(
        obs_values.reshape(n_patch, n_lat, capacity, breadth),
        obs_node.reshape(n_patch, n_lat, capacity, OBS_EDGES),
        obs_count.reshape(n_patch, n_lat),
    )
    arrived = arrived.reshape(senders * capacity, breadth)
    targets = targets.reshape(senders * capacity, OBS_EDGES)
    embedded = embed_rows(arrived, w_in)
    alive = (
        (jnp.arange(capacity, dtype=jnp.int32)[None, :] < counts.reshape(senders, 1))
        .astype(jnp.float32)
        .reshape(-1)
    )
    encoded = jnp.dot(mesh_init, w_enc, preferred_element_type=jnp.float32)
    query = encoded[:, :D] + edge_bias[0]
    total_rows = senders * capacity
    block = min(512, total_rows)
    turns = total_rows // block
    node_ids = jnp.arange(node_dev, dtype=jnp.int32)[None, :]

    def encode_block(block_index, totals):
        start = block_index * block
        piece = lax.dynamic_slice_in_dim(embedded, start, block, 0).astype(jnp.float32)
        nodes = lax.dynamic_slice_in_dim(targets, start, block, 0)
        weight = lax.dynamic_slice_in_dim(alive, start, block, 0)[:, None]
        for which in range(OBS_EDGES):
            selector = (nodes[:, which][:, None] == node_ids).astype(jnp.float32)
            picked = jnp.dot(selector, query, precision=lax.Precision.HIGHEST)
            message = jax.nn.silu(piece + picked) * weight
            totals = totals + lax.dot_general(
                selector, message, (((0,), (0,)), ((), ())), precision=lax.Precision.HIGHEST
            )
        return totals

    totals = lax.fori_loop(0, turns, encode_block, jnp.zeros((node_dev, D), jnp.float32))
    gathered = totals.astype(jnp.bfloat16)
    hidden = jax.nn.silu(
        encoded[:, D:] + jnp.dot(gathered, w_agg, preferred_element_type=jnp.float32) + node_bias[0]
    ).astype(jnp.bfloat16)
    first = (
        mesh_init.astype(jnp.float32)
        + layer_norm(jnp.dot(hidden, w_out, preferred_element_type=jnp.float32), norm_gain[0])
    ).astype(jnp.bfloat16)
    projected = jnp.dot(first, w_proc, preferred_element_type=jnp.float32)
    sources = projected[:, :D].astype(jnp.bfloat16)
    target = projected[:, D : 2 * D] + edge_bias[1]
    padded = extended(sources, ((("patch", "lat"), 0),), HALO)
    local_ids = jnp.arange(node_dev, dtype=jnp.int32) + HALO
    pooled = jnp.zeros((node_dev, D), jnp.float32)
    for which in range(DEG):
        anchor = local_ids + mesh_offset[:, which]
        pooled = pooled + jax.nn.silu(jnp.take(padded, anchor, axis=0).astype(jnp.float32) + target)
    hidden2 = jax.nn.silu(
        projected[:, 2 * D :]
        + jnp.dot(pooled.astype(jnp.bfloat16), w_pagg, preferred_element_type=jnp.float32)
        + node_bias[1]
    ).astype(jnp.bfloat16)
    return (
        first.astype(jnp.float32)
        + layer_norm(jnp.dot(hidden2, w_pout, preferred_element_type=jnp.float32), norm_gain[1])
    ).astype(jnp.bfloat16)


BF = jnp.bfloat16
F32 = jnp.float32
TILE = 16
FRAME = 176
DEAD = 256.0


def silu(values):
    half = 0.5 * values
    return half + half * jnp.tanh(half)


def mm(left, right):
    return jnp.dot(left, right, preferred_element_type=F32)


def iota(shape, dim):
    return lax.broadcasted_iota(jnp.int32, shape, dim)


def in_vmem():
    return pl.BlockSpec(memory_space=pltpu.VMEM)


def in_smem():
    return pl.BlockSpec(memory_space=pltpu.SMEM)


def in_any():
    return pl.BlockSpec(memory_space=pltpu.HBM)


def frame_kernel(me_ref, *refs):
    outs = refs[4:6]
    w_ref, val_ref, node_ref, count_ref, turned, slots, rows, frame, sems = refs[6:]
    copies = [
        pltpu.make_async_copy(src, dst, sems.at[i])
        for i, (src, dst) in enumerate(zip(refs[:4], (w_ref, val_ref, node_ref, count_ref)))
    ]
    for copy in copies:
        copy.start()
    for copy in copies:
        copy.wait()
    me = me_ref[0]
    breadth, n_slots = val_ref.shape
    senders = count_ref.shape[1]
    capacity = n_slots // senders
    phase = lax.rem(WROWS * me, TILE)
    for r in range(WROWS):
        frame[pl.ds(phase + r, 1), :] = w_ref[0:1, D * r : D * (r + 1)].astype(F32)
    own = (iota((senders, n_slots), 0) == iota((senders, n_slots), 1) // capacity).astype(BF)
    counts = jnp.broadcast_to(count_ref[...], (8, senders)).astype(F32).astype(BF)
    live = mm(counts, own)[0:1, :]
    place = (iota((1, n_slots), 1) % capacity).astype(F32)
    code = jnp.where(place < live, node_ref[...].astype(F32) - DEAD, DEAD)
    turned[:breadth, :] = val_ref[...].astype(F32)
    feature = iota((n_slots - breadth, n_slots), 0)
    tail = jnp.zeros((n_slots - breadth, n_slots), F32)
    for k in range(OBS_EDGES):
        tail = jnp.where(feature == k, code[k : k + 1, :], tail)
    turned[breadth:, :] = tail
    slots[...] = turned[...].T
    for j in range(capacity):
        rows[:, 128 * j : 128 * (j + 1)] = slots[pl.ds(j, senders, stride=capacity), :]
    start = pl.multiple_of(jnp.where(phase >= 8, 0, FRAME - 16), 8)
    lane = iota((8, 128), 1)
    line = iota((8, 128), 0)
    used = breadth + OBS_EDGES
    quarter = breadth // capacity

    def block(plane):
        before = slots[pl.ds(pl.multiple_of(lax.rem(32 * plane + 120, 128), 8), 8), :]
        after = slots[pl.ds(pl.multiple_of(lax.rem(32 * plane + 32, 128), 8), 8), :]
        extra = pltpu.roll(jnp.where(line < 4, after, before), 4, 0)
        base = rows[pl.ds(pl.multiple_of(8 * plane, 8), 8), :]
        parts = []
        for g in range(capacity):
            moved = pltpu.roll(extra, (used - quarter * g) % 128, 1)
            keep = (lane >= used) & (lane < used + quarter)
            parts.append(jnp.where(keep, moved, base[:, 128 * g : 128 * (g + 1)]))
        keep = (lane >= used + quarter) & (lane < used + quarter + OBS_EDGES)
        parts[0] = jnp.where(keep, pltpu.roll(extra, used + quarter - breadth, 1), parts[0])
        return jnp.concatenate(parts, axis=1)

    for flip in range(2):
        frame[pl.ds(start, 8), :] = block((me >> 3) ^ (2 * flip))
        frame[FRAME - 8 :, :] = block((me >> 3) ^ (2 * flip + 1))
        outs[flip][...] = frame[...].astype(BF)


def layer_kernel(me_ref, *refs):
    pieces = refs[:16]
    low_ref, init_ref, high_ref, off_ref, edge_ref, nbias_ref, gain_ref, out_ref = refs[16:24]
    big, edges, obs, enc, proc, ext, wide = refs[24:]
    count = init_ref.shape[0]
    height = WROWS
    me = me_ref[0]
    core = me & 1
    for unit in range(4):
        for twin in range(2):
            ax = jnp.where((core ^ twin) == 0, 4, 2)
            ay = jnp.where((core ^ twin) == 0, 2, 4)
            for pair in range(2):
                for j in range(2):
                    piece = pieces[unit * 4 + twin * 2 + pair]
                    mask = (8 * unit) ^ twin ^ (ax if j else 0) ^ (ay if pair else 0)
                    dev = me ^ mask
                    row = pl.multiple_of((height * dev) // TILE * TILE + TILE, TILE)
                    edges[dev, 0:TILE, :] = piece[j, 0:TILE, :]
                    big[pl.ds(row, 128), :] = piece[j, TILE : TILE + 128, :]
                    edges[dev, TILE : 3 * TILE, :] = piece[j, 144:FRAME, :]
                    if unit % 2:
                        spot = jnp.where(lax.rem(height * dev, TILE) >= 8, 0, 32)
                        edges[dev, pl.ds(pl.multiple_of(spot, TILE), 8), :] = piece[j, FRAME - 8 :, :]
    row16 = iota((TILE, D), 0)
    for dev in range(32):
        phase = height * dev % TILE
        tile = height * dev // TILE
        after = height * (dev + 1) // TILE
        head = edges[dev, 0:TILE, :]
        if phase:
            before = height * (dev - 1) // TILE
            skip = TILE * (tile - before) - 144
            last = edges[dev - 1, TILE + skip : 2 * TILE + skip, :]
            head = jnp.where(row16 < phase, last.astype(F32), head.astype(F32)).astype(BF)
        big[TILE * tile : TILE * (tile + 1), :] = head
        if after - tile == 10:
            big[TILE * (tile + 9) : TILE * (tile + 10), :] = edges[dev, TILE : 2 * TILE, :]
        if phase >= 8:
            seen = edges[dev, 0:TILE, :].astype(F32)[0:8]
        else:
            seen = edges[dev, 2 * TILE : 3 * TILE, :].astype(F32)[0:8]
        for j in range(4):
            obs[j, 8 * dev : 8 * (dev + 1), :] = seen[:, 128 * j : 128 * (j + 1)]
    e0 = CH
    a0 = CH + 2 * D
    o0 = CH + 3 * D
    p0 = CH + 4 * D
    g0 = CH + 7 * D
    u0 = CH + 8 * D

    def unfold(base, fold, dest, j):
        lanes = slice(128 * j, 128 * (j + 1))
        wide[j, 0 : fold * D, :] = big[base : base + fold * D, lanes].astype(F32)
        for m in range(fold):
            dest[m, :, lanes] = wide[j, pl.ds(m, D, stride=fold), :].astype(BF)

    out = iota((256, 256), 0)
    two = (iota((256, 256), 1) == 2 * (out & 127) + (out >> 7)).astype(BF)
    for j in range(D // 128):
        got = mm(two, big[e0 + 256 * j : e0 + 256 * (j + 1), :]).astype(BF)
        enc[0, 128 * j : 128 * (j + 1), :] = got[:128]
        enc[1, 128 * j : 128 * (j + 1), :] = got[128:]
        if j == 1:
            unfold(p0, 3, proc, 0)
    init = jnp.concatenate([low_ref[...], init_ref[...], high_ref[...]], axis=0)
    query = (mm(init, enc[0]) + edge_ref[0:1, :]).astype(BF)
    spot = me & 7
    lane = iota((32, 128), 1)
    used = CH + OBS_EDGES
    quarter = CH // 4

    def direct(row):
        return jnp.concatenate([obs[j, pl.ds(row, 32, stride=8), :] for j in range(4)], axis=0)

    def spilled(row):
        groups = []
        for j in range(4):
            near = obs[0, pl.ds(row + j, 32, stride=8), :]
            slot = pltpu.roll(near, (CH - used - quarter) % 128, 1)
            for g in range(4):
                part = near if g == 0 else obs[g, pl.ds(row + j, 32, stride=8), :]
                keep = (lane >= quarter * g) & (lane < quarter * (g + 1))
                slot = jnp.where(keep, pltpu.roll(part, (quarter * g - used) % 128, 1), slot)
            groups.append(slot)
        return jnp.concatenate(groups, axis=0)

    before = jnp.where(spot > 0, direct(jnp.maximum(spot - 1, 0)), spilled(0))
    after = jnp.where(spot < 7, direct(jnp.minimum(spot + 1, 7)), spilled(4))
    rows = [before, direct(spot), after]
    per = rows[0].shape[0]
    joined = jnp.concatenate(rows, axis=0)
    embedded = mm(joined[:, :CH].astype(BF), big[0:CH, :]).astype(BF).astype(F32)
    sums = []
    for part, shift, top, size in (
        (0, count - HALO, 0, HALO),
        (1, 0, HALO, count),
        (2, 0, HALO + count, HALO),
    ):
        slots = rows[part]
        embeds = embedded[per * part : per * (part + 1)]
        node_ids = iota((slots.shape[0], size), 1)
        picks = []
        for k in range(OBS_EDGES):
            code = slots[:, CH + k : CH + k + 1] + (DEAD - shift)
            picks.append((node_ids == code.astype(jnp.int32)).astype(F32))
        select = jnp.concatenate(picks, axis=0)
        picked = mm(select.astype(BF), query[top : top + size])
        message = silu(jnp.concatenate([embeds] * OBS_EDGES, axis=0) + picked)
        sums.append(mm(select.T.astype(BF), message.astype(BF)).astype(BF))
        unfold(p0, 3, proc, part + 1)
    gathered = jnp.concatenate(sums, axis=0)
    hidden = silu(
        mm(init, enc[1]) + mm(gathered, big[a0 : a0 + D, :]) + nbias_ref[0:1, :]
    ).astype(BF)
    first = (
        init.astype(F32) + layer_norm(mm(hidden, big[o0 : o0 + D, :]), gain_ref[0:1, :])
    ).astype(BF)
    ext[...] = mm(first, proc[0]).astype(BF)
    first = first[HALO : HALO + count]
    block = count // 2
    span = block + 2 * HALO
    cols = iota((block, span), 1) - iota((block, span), 0) - HALO
    target = 0.5 * (mm(first, proc[1]) + edge_ref[1:2, :])
    sums = []
    for at in range(0, count, block):
        select = jnp.concatenate(
            [jnp.where(cols == off_ref[at : at + block, k : k + 1], 0.5, 0.0) for k in range(DEG)], axis=0
        ).astype(BF)
        picked = mm(select, ext[at : at + span, :])
        base = target[at : at + block]
        total = jnp.zeros((block, D), F32)
        for k in range(DEG):
            half = picked[block * k : block * (k + 1)] + base
            total = total + (half + half * jnp.tanh(half))
        sums.append(total)
    pooled = jnp.concatenate(sums, axis=0).astype(BF)
    hidden = silu(
        mm(first, proc[2]) + nbias_ref[1:2, :] + mm(pooled, big[g0 : g0 + D, :])
    ).astype(BF)
    out_ref[...] = (
        first.astype(F32) + layer_norm(mm(hidden, big[u0 : u0 + D, :]), gain_ref[1:2, :])
    ).astype(BF)


WROWS = 147


def fits(obs_values, mesh_init, weights_flat):
    return (
        lax.axis_size("patch") == 8
        and lax.axis_size("lat") == 4
        and weights_flat.shape[1] == WROWS * D
        and obs_values.shape == (128, CH)
        and mesh_init.shape[0] <= 320
        and mesh_init.shape[0] >= HALO
        and mesh_init.shape[0] % 32 == 0
    )


def spread_weights(near, far, init):
    axes = ("patch", "lat")
    count = init.shape[0]
    ring = [(i, (i + 1) % 32) for i in range(32)]

    def move(block, masks):
        return lax.ppermute(block, axes, [(i, i ^ masks[i & 1]) for i in range(32)])

    low = lax.ppermute(init[count - HALO :], axes, ring)
    high = lax.ppermute(init[:HALO], axes, [(j, i) for i, j in ring])
    beside = move(near, (4, 2))
    opposite = move(far, (16, 16))
    aside = move(opposite, (4, 2))
    pieces = []
    for unit, twin in (
        (near, beside),
        (move(near, (8, 8)), move(beside, (8, 8))),
        (opposite, aside),
        (move(opposite, (8, 8)), move(aside, (8, 8))),
    ):
        pair = jnp.stack([unit, twin])
        other = move(pair, (2, 4))
        pieces += [pair, other, move(pair, (1, 1)), move(other, (1, 1))]
    return pieces + [low, init, high]


def shards(
    obs_values,
    obs_count,
    obs_node,
    mesh_init,
    mesh_offset,
    weights_flat,
    edge_bias,
    node_bias,
    norm_gain,
):
    if not fits(obs_values, mesh_init, weights_flat):
        return general(
            obs_values,
            obs_count,
            obs_node,
            mesh_init,
            mesh_offset,
            weights_flat,
            edge_bias,
            node_bias,
            norm_gain,
        )
    axes = ("patch", "lat")
    me = lax.axis_index(axes).astype(jnp.int32).reshape(1)
    count = mesh_init.shape[0]
    frames = pl.pallas_call(
        frame_kernel,
        out_shape=[jax.ShapeDtypeStruct((FRAME, D), BF)] * 2,
        in_specs=[in_smem()] + [in_any()] * 4,
        out_specs=[in_vmem()] * 2,
        scratch_shapes=[
            pltpu.VMEM(weights_flat.shape, BF),
            pltpu.VMEM(obs_values.shape[::-1], BF),
            pltpu.VMEM(obs_node.shape[::-1], jnp.int32),
            pltpu.VMEM(obs_count.shape, jnp.int32),
            pltpu.VMEM((128, 128), F32),
            pltpu.VMEM((128, 128), F32),
            pltpu.VMEM((32, D), F32),
            pltpu.VMEM((FRAME, D), F32),
            pltpu.SemaphoreType.DMA((4,)),
        ],
        compiler_params=pltpu.CompilerParams(vmem_limit_bytes=60 << 20),
        name="frames",
    )(me, weights_flat, obs_values.T, obs_node.T, obs_count)
    pieces = spread_weights(*frames, mesh_init)
    return pl.pallas_call(
        layer_kernel,
        out_shape=jax.ShapeDtypeStruct((count, D), BF),
        in_specs=[in_smem()] + [in_vmem()] * 23,
        out_specs=in_vmem(),
        scratch_shapes=[
            pltpu.VMEM((32 * WROWS, D), BF),
            pltpu.VMEM((32, 3 * TILE, D), BF),
            pltpu.VMEM((4, 256, 128), F32),
            pltpu.VMEM((2, D, D), BF),
            pltpu.VMEM((3, D, D), BF),
            pltpu.VMEM((count + 2 * HALO, D), BF),
            pltpu.VMEM((4, 3 * D, 128), F32),
        ],
        compiler_params=pltpu.CompilerParams(vmem_limit_bytes=40 << 20),
        name="layer",
    )(me, *pieces, mesh_offset, edge_bias, node_bias, norm_gain)


def solution(mesh):
    return jax.shard_map(
        shards,
        mesh=mesh,
        in_specs=(
            P(("patch", "lat"), None),
            P(("patch", "lat"), None),
            P(("patch", "lat"), None),
            P(("patch", "lat"), None),
            P(("patch", "lat"), None),
            P(("patch", "lat"), None),
            P(),
            P(),
            P(),
        ),
        out_specs=P(("patch", "lat"), None),
        check_vma=False,
    )
```
